256 devices in a mesh: tm: 16 (over z, core), lon: 8 (over y, x_lo), ens: 2 (over x_hi).
Axes of the slice: x: 4 (x_hi: 2, x_lo: 2; x = x_hi * 2 + x_lo), y: 4, z: 8, core: 2. Of those that a mesh axis runs over, the one named last changes fastest.
Arguments:
- anomalies: bfloat16 [8192, 1024], P('lon', 'ens'), may hold values from -6 to 6
- localization: bfloat16 [64, 3, 128, 128], P('lon'), may hold values from -0.3125 to 0.3125
- innovations: float32 [16, 4096], P('tm', 'lon'), may hold values from -6 to 6
- obs_cell: int32 [16, 4096], P('tm', 'lon'), may hold values from 0 to 1023
- tangent_blocks: float32 [16, 8, 128, 128], P('tm'), may hold values from -1 to 2
- tangent_order: int32 [16, 8], P('tm'), may hold values from 0 to 7, each once within a row
Outputs:
- forward_states: float32 [16, 1024, 1024], P('tm', ('ens', 'lon'))
- adjoint_states: float32 [16, 1024, 1024], P('tm', ('ens', 'lon'))
The draws below stay inside these ranges and needn't reach their ends.
Inputs may be any that keep to these rules, and one draw needn't show every extreme that they name: Observation j of a step lies in sector j // 512, at that sector's cell obs_cell. `tangent_order`: each step's row names every block index once.
All inputs are finite; a program needn't handle non-finite values.
Results may differ from the reference program's by a relative error of at most 0.015.
Values may be sent and summed in bfloat16 or wider, within the bound.
No kernel may reach another device: no remote copies, remote signals or barrier semaphores. Data moves between devices by JAX's collectives and lax.ppermute only.
A program may use at most 64 MiB of HBM per device.

```python
import math
import jax
import jax.numpy as jnp
from jax import lax

R = 1024
BLK = 128
CELLS_DEV = 1024
OBS_DEV = 512
MAP_PIECES = 8
CYCLE_INCREMENTS = 16
NCELL = 8192
NCB = 64
NOBS = 4096
N_LON = 8


def draw_tangent_blocks(key, part):
    perturbation_random_start, gradual_random_start, spike_random_start, wobble_random_start = jax.random.split(key, 4)
    identity = jnp.eye(BLK, dtype=jnp.float32)
    noise = jnp.clip(jax.random.normal(perturbation_random_start, (CYCLE_INCREMENTS, MAP_PIECES, BLK, BLK), jnp.float32), -4.0, 4.0) * (0.25 / math.sqrt(BLK))
    slow = jax.random.uniform(gradual_random_start, (MAP_PIECES,), jnp.float32) < 0.5
    slow_rate = math.log(0.3) / CYCLE_INCREMENTS - 0.03
    fast_rate = -1.0 / 40.0 - 0.03
    damping_speed = jnp.where(slow, slow_rate, fast_rate)
    wobble_magnitude = jax.random.uniform(wobble_random_start, (CYCLE_INCREMENTS, MAP_PIECES), jnp.float32, 0.7, 1.4)
    spike_magnitude = jnp.where(jax.random.uniform(spike_random_start, (CYCLE_INCREMENTS, MAP_PIECES), jnp.float32) < 3.0 / CYCLE_INCREMENTS, 0.6, 1.0)
    growth_multiplier = jnp.exp(damping_speed[None, :] * wobble_magnitude) * spike_magnitude
    return (growth_multiplier[:, :, None, None] * (identity + noise)).astype(jnp.float32)


def with_ends(entries, own_key, smallest, largest):
    shape = entries.shape
    index_at = [jax.random.randint(jax.random.fold_in(own_key, axis), (), 0, shape[axis]) for axis in range(len(shape))]
    entries = entries.at[tuple(index_at)].set(smallest)
    longest = shape.index(max(shape))
    index_at[longest] = (index_at[longest] + 1) % shape[longest]
    return entries.at[tuple(index_at)].set(largest)


def levels(rng, extent, shards, low, high):
    def one(position, shards_of):
        draws = jax.random.uniform(jax.random.fold_in(jax.random.fold_in(rng, 6), position), (shards_of,), jnp.float32, low / len(shards), high / len(shards))
        return jnp.repeat(jnp.exp(draws), extent[position] // shards_of).reshape((-1,) + (1,) * (len(extent) - position - 1))

    gain = one(*shards[0])
    for cut in shards[1:]:
        gain = gain * one(*cut)
    return gain


def normal_values(stream_key, extent, width, limit, cuts=(), kind=jnp.bfloat16):
    loudness = levels(stream_key, extent, cuts, -0.22, 0.18) if cuts else 1.0
    result = jax.random.normal(stream_key, extent, jnp.float32) * width * loudness
    return jnp.minimum(jnp.maximum(result, -limit), limit).astype(kind)


def setup_inputs(seed: int = 0) -> dict:
    seeds = jax.random.split(jax.random.key(seed), 7)
    anomalies = normal_values(seeds[0], (NCELL, R), 1.0, 6.0, ((0, 8), (1, 2)))
    localization = normal_values(seeds[1], (NCB, 3, BLK, BLK), (3 * BLK) ** -0.5, 0.3125, ((0, 8),))
    innovations = normal_values(seeds[2], (CYCLE_INCREMENTS, NOBS), 1.0, 6.0, ((0, 16), (1, 8)), jnp.float32)
    obs_cell = with_ends(jax.random.randint(seeds[3], (CYCLE_INCREMENTS, NOBS), 0, CELLS_DEV), jax.random.fold_in(seeds[3], 1), 0, CELLS_DEV - 1).astype(jnp.int32)
    tangent_blocks = draw_tangent_blocks(jax.random.fold_in(seeds[6], 71), 0)
    tangent_order = jax.vmap(lambda own: jax.random.permutation(own, MAP_PIECES))(jax.random.split(seeds[5], CYCLE_INCREMENTS)).reshape((CYCLE_INCREMENTS, MAP_PIECES)).astype(jnp.int32)
    return {"anomalies": anomalies, "localization": localization, "innovations": innovations, "obs_cell": obs_cell, "tangent_blocks": tangent_blocks, "tangent_order": tangent_order}


precise_mode = lax.Precision.HIGHEST


def apply_forward(blocks, order, state):
    row_count = state.shape[0]
    split_point = state.reshape(row_count, MAP_PIECES, BLK)
    chosen = jnp.take(split_point, order, axis=1)
    return jnp.einsum('mic,idc->mid', chosen, blocks, precision=precise_mode).reshape(row_count, R)


def apply_adjoint(blocks, order, state):
    row_count = state.shape[0]
    split_point = state.reshape(row_count, MAP_PIECES, BLK)
    moved = jnp.einsum('mic,icd->mid', split_point, blocks, precision=precise_mode)
    placed = jnp.zeros_like(moved).at[:, order, :].set(moved)
    return placed.reshape(row_count, R)


def localize(weighted, localization):
    padded = jnp.concatenate([weighted[NCELL - BLK:], weighted, weighted[:BLK]], axis=0).astype(jnp.float32)
    stacked = padded.reshape(NCB + 2, BLK, R)
    local_ops = localization.astype(jnp.float32)
    total = jnp.zeros((NCB, BLK, R), jnp.float32)
    for offset in range(3):
        total = total + jnp.einsum('bij,bjm->bim', local_ops[:, offset], stacked[offset:offset + NCB], precision=precise_mode)
    return total.reshape(NCELL, R).astype(jnp.bfloat16)


def reference(anomalies, localization, innovations, obs_cell, tangent_blocks, tangent_order):
    scale = float(NCELL) ** -0.5
    sectors = (jnp.arange(NOBS, dtype=jnp.int32) // OBS_DEV).astype(jnp.int32)
    anomaly_float = anomalies.astype(jnp.float32)

    def forcing_step(inputs):
        innov_row, cell_row = inputs
        where_cells = (sectors * CELLS_DEV + cell_row).astype(jnp.int32)
        obs_weight = jnp.zeros((NCELL,), jnp.float32).at[where_cells].add(innov_row)
        weighted = (obs_weight[:, None] * anomaly_float).astype(jnp.bfloat16)
        localized = localize(weighted, localization)
        sector_loc = localized.astype(jnp.float32).reshape(N_LON, CELLS_DEV, R)
        sector_anom = anomaly_float.reshape(N_LON, CELLS_DEV, R)
        partial_sums = (jnp.einsum('scm,scr->smr', sector_loc, sector_anom, precision=precise_mode) * scale).astype(jnp.bfloat16)
        return jnp.sum(partial_sums.astype(jnp.float32), axis=0)

    forcing = lax.map(forcing_step, (innovations, obs_cell))

    def forward_turn(state, inputs):
        blocks, order, force = inputs
        state = apply_forward(blocks, order, state) + force
        return state, state

    def adjoint_turn(state, inputs):
        blocks, order, force = inputs
        state = apply_adjoint(blocks, order, state + force)
        return state, state

    start = jnp.zeros((R, R), jnp.float32)
    forward_states = lax.scan(forward_turn, start, (tangent_blocks, tangent_order, forcing))[1]
    adjoint_states = lax.scan(adjoint_turn, start, (tangent_blocks, tangent_order, forcing), reverse=True)[1]
    return forward_states, adjoint_states
```

```python
import functools

import jax
import jax.numpy as jnp
from jax import lax
from jax.experimental import pallas as pl
from jax.experimental.pallas import tpu as pltpu
from jax.sharding import Mesh
from jax.sharding import PartitionSpec as P

BLK = 128
NB = 8
COLS = NB * BLK
bf16 = jnp.bfloat16
f32 = jnp.float32

VM = pl.BlockSpec(memory_space=pltpu.VMEM)
SM = pl.BlockSpec(memory_space=pltpu.SMEM)
ANY = pl.BlockSpec(memory_space=pl.ANY)

MSG = COLS + 16
HALF = COLS // 2 + 16
PACK = 3 * MSG + HALF


def call(kernel, outs, ins, scratch=(), flops=0, data=0):
    return pl.pallas_call(
        kernel,
        out_shape=outs,
        in_specs=ins,
        out_specs=[VM] * len(outs),
        scratch_shapes=list(scratch),
        compiler_params=pltpu.CompilerParams(vmem_limit_bytes=48 * 1024 * 1024),
        cost_estimate=pl.CostEstimate(flops=flops, bytes_accessed=data, transcendentals=0),
    )


def split(x):
    hi = x.astype(bf16)
    lo = (x - hi.astype(f32)).astype(bf16)
    return jnp.concatenate([hi, lo], axis=0)


def times(x, block, transposed):
    dims = (((1,), (1,)), ((), ())) if transposed else (((1,), (0,)), ((), ()))
    y = lax.dot_general(split(x), block, dims, preferred_element_type=f32)
    rows = x.shape[0]
    return y[:rows] + y[rows:]


def cols_at(i):
    return pl.ds(pl.multiple_of(i * BLK, BLK), BLK)


def weight_kernel(innov, cell, anom, out):
    cells = anom.shape[0]
    step = 256
    for c in range(0, cells, step):
        ids = lax.broadcasted_iota(jnp.int32, (step, 1), 0) + c
        hit = jnp.where(ids == cell[...], innov[...], 0.0)
        w = jnp.sum(hit, axis=1, keepdims=True)
        out[pl.ds(c, step), :] = (w * anom[pl.ds(c, step), :].astype(f32)).astype(bf16)


def local_kernel(scale, before, mid, after, loc, anom, lout, pout, pad):
    n = mid.shape[0]
    pad[:BLK] = before[...]
    pad[BLK : BLK + n] = mid[...]
    pad[BLK + n :] = after[...]
    for b in range(n // BLK):
        left = jnp.concatenate([loc[b, 0], loc[b, 1], loc[b, 2]], axis=1)
        y = jnp.dot(left, pad[b * BLK : b * BLK + 3 * BLK], preferred_element_type=f32)
        lout[b * BLK : (b + 1) * BLK] = y.astype(bf16)
    y = lax.dot_general(lout[...], anom[...], (((0,), (0,)), ((), ())), preferred_element_type=f32)
    pout[...] = (y * scale).astype(bf16)


def other_kernel(scale, lin, near, far, pout):
    co = lax.axis_index("co")
    n = near.shape[0]
    dims = (((0,), (0,)), ((), ()))
    mine = lin[pl.ds(pl.multiple_of(co * n, n), n), :]
    rest = lin[pl.ds(pl.multiple_of((1 - co) * n, n), n), :]
    y = lax.dot_general(mine, near[...], dims, preferred_element_type=f32)
    y = y + lax.dot_general(rest, far[...], dims, preferred_element_type=f32)
    pout[...] = (y * scale).astype(bf16)


def map_kernel(own, oth, ords, both, comp):
    co = lax.axis_index("co")
    both[co] = own[:COLS]
    both[1 - co] = oth[:COLS]
    row = lax.broadcasted_iota(jnp.int32, (16, BLK), 1)
    tag = jnp.zeros((16, BLK), f32)
    for i in range(NB):
        k = ords[1, i]
        low = both[0, pl.ds(pl.multiple_of(k * BLK, BLK), BLK), :]
        y = jnp.dot(both[1, i * BLK : (i + 1) * BLK], low, preferred_element_type=f32)
        comp[i * BLK : (i + 1) * BLK] = y.astype(bf16)
        tag = jnp.where(row == i, ords[0, k].astype(f32), tag)
    comp[COLS:] = tag.astype(bf16)


def sum_kernel(first, second, own, send, acc):
    co = lax.axis_index("co")
    e = lax.axis_index("ens")
    rows = acc.shape[0]
    half = first.shape[1]
    for src, place in ((first, e), (second, 1 - e)):
        y = src[:rows].astype(f32)
        for s in range(1, src.shape[0] // rows):
            y = y + src[s * rows : (s + 1) * rows].astype(f32)
        acc[:, pl.ds(pl.multiple_of(place * half, half), half)] = y
    h = rows // 2
    own[...] = acc[pl.ds(pl.multiple_of(co * h, h), h), :]
    send[...] = acc[pl.ds(pl.multiple_of((1 - co) * h, h), h), :].astype(bf16)


def total_kernel(own, oth, both, ords, out, force, tmp, tot):
    co = lax.axis_index("co")
    z = lax.axis_index("z")
    force[co] = own[...]
    force[1 - co] = oth[...].astype(f32)
    for i in range(NB):
        blk = both[1, i * BLK : (i + 1) * BLK]
        k = ords[1, i]
        y = times(force[0, :, cols_at(k)], blk, True)
        tot[0, :, i * BLK : (i + 1) * BLK] = y + force[1, :, i * BLK : (i + 1) * BLK]
        tmp[:, cols_at(k)] = times(force[1, :, i * BLK : (i + 1) * BLK], blk, False)
    tmp[...] = tmp[...] + force[0]
    for i in range(NB):
        blk = both[0, i * BLK : (i + 1) * BLK]
        tot[1, :, cols_at(ords[0, i])] = times(tmp[:, i * BLK : (i + 1) * BLK], blk, False)
    fwd = tot[0].astype(bf16)
    adj = tot[1].astype(bf16)
    for d in range(out.shape[0]):
        out[d] = jnp.where(d > z, fwd, adj)


def sweep_kernel(recv, mine, theirs, tags, both, ords, own, oth, keep, send, maps, sem, st, adj, force, res):
    co = lax.axis_index("co")
    z = lax.axis_index("z")
    c0 = pltpu.make_async_copy(mine, maps.at[co], sem.at[0])
    c1 = pltpu.make_async_copy(theirs, maps.at[1 - co], sem.at[1])
    c0.start()
    c1.start()
    force[co] = own[...]
    force[1 - co] = oth[...].astype(f32)
    nz = recv.shape[0]
    st[0] = jnp.where(z > 0, recv[0].astype(f32), 0.0)
    adj[0] = jnp.where(z < nz - 1, recv[nz - 1].astype(f32), 0.0)
    c0.wait()
    c1.wait()

    def where_is(k, i):
        d = lax.rem(k - z + nz, nz)
        core = jnp.where(d < 4, 0, jnp.where(d > 4, 1, i // 4))
        slot = jnp.where(d < 4, d - 1, jnp.where(d > 4, 7 - d, 3))
        off = jnp.where(d == 4, i % 4, i)
        return core, slot, pl.multiple_of(slot * MSG + off * BLK, 16)

    def forward(k, cur):
        src, dst = cur, 1 - cur
        for i in range(NB):
            core, slot, row = where_is(k, i)
            blk = maps[core, pl.ds(row, BLK), :]
            o = tags[jnp.where(core == co, 0, 1), slot, i]
            y = times(st[src, :, cols_at(o)], blk, True)
            st[dst, :, i * BLK : (i + 1) * BLK] = y + recv[k, :, i * BLK : (i + 1) * BLK].astype(f32)
        return dst

    def backward(s, cur):
        k = nz - 1 - s
        src, dst = cur, 1 - cur
        for i in range(NB):
            core, slot, row = where_is(k, i)
            blk = maps[core, pl.ds(row, BLK), :]
            o = tags[jnp.where(core == co, 0, 1), slot, i]
            y = times(adj[src, :, i * BLK : (i + 1) * BLK], blk, False)
            adj[dst, :, cols_at(o)] = y + recv[k, :, cols_at(o)].astype(f32)
        return dst

    cf = lax.fori_loop(1, z, forward, jnp.int32(0))
    cb = lax.fori_loop(1, nz - 1 - z, backward, jnp.int32(0))
    for t in range(2):
        for i in range(NB):
            cols = slice(i * BLK, (i + 1) * BLK)
            o = cols_at(ords[t, i])
            x = st[cf, :, o] if t == 0 else res[0, 0, :, o]
            res[t, 0, :, cols] = times(x, both[t, cols], True) + force[t, :, cols]
            u = 1 - t
            o = cols_at(ords[u, i])
            y = adj[cb, :, cols] if u == 1 else res[1, 1, :, cols]
            res[u, 1, :, o] = times(y + force[u, :, cols], both[u, cols], False)
    keep[...] = res[co]
    send[...] = res[1 - co].astype(bf16)


def on_device(anomalies, localization, innovations, obs_cell, tangent_blocks, tangent_order):
    cells, half_cols = anomalies.shape
    n_lon = lax.axis_size("lon")
    nz = lax.axis_size("z")
    co = lax.axis_index("co")
    shape = jax.ShapeDtypeStruct
    swap = [(0, 1), (1, 0)]
    scale = float(cells * n_lon) ** (-0.5)

    h = cells // 2
    piece = lax.dynamic_slice_in_dim(anomalies, co * h, h, 0)
    near = lax.ppermute(piece, "ens", swap)

    order_own = tangent_order[0]
    tag = jnp.zeros((16, BLK), f32).at[0, :NB].set(order_own.astype(f32))
    own_map = jnp.concatenate([tangent_blocks.reshape(COLS, BLK), tag], axis=0).astype(bf16)
    oth_map = lax.ppermute(own_map, "co", swap)

    (weighted,) = call(weight_kernel, [shape((cells, half_cols), bf16)], [VM] * 3, flops=10**6, data=2 * 10**6)(
        innovations, obs_cell, anomalies
    )
    up = [(i, (i + 1) % n_lon) for i in range(n_lon)]
    down = [(b, a) for a, b in up]
    before = lax.ppermute(weighted[cells - BLK :], "lon", up)
    after = lax.ppermute(weighted[:BLK], "lon", down)

    order_oth = oth_map[COLS, :NB].astype(jnp.int32)
    ords = jnp.where(co == 0, jnp.stack([order_own, order_oth]), jnp.stack([order_oth, order_own]))
    both, comp = call(
        map_kernel, [shape((2, COLS, BLK), bf16), shape((MSG, BLK), bf16)], [VM, VM, SM], flops=10**7, data=10**6
    )(own_map, oth_map, ords)

    got = []
    for d in range(1, 4):
        pairs = []
        for k in range(nz):
            pairs.append((((k + d) % nz) * 2, k * 2))
            pairs.append((((k - d) % nz) * 2 + 1, k * 2 + 1))
        got.append(lax.ppermute(comp, ("z", "co"), pairs))
    part = jnp.concatenate([lax.dynamic_slice_in_dim(comp, co * (COLS // 2), COLS // 2, 0), comp[COLS:]], axis=0)
    got.append(lax.ppermute(part, "z", [((k + nz // 2) % nz, k) for k in range(nz)]))

    local, p_own = call(
        functools.partial(local_kernel, scale),
        [shape((cells, half_cols), bf16), shape((half_cols, half_cols), bf16)],
        [VM] * 5,
        [pltpu.VMEM((cells + 2 * BLK, half_cols), bf16)],
        flops=10**9,
        data=4 * 10**6,
    )(before, weighted, after, localization, anomalies)
    first = lax.all_to_all(p_own, "lon", 0, 0, tiled=True)
    near, first = lax.optimization_barrier((near, first))
    far = lax.ppermute(near, "co", swap)
    (p_oth,) = call(
        functools.partial(other_kernel, scale), [shape((half_cols, half_cols), bf16)], [VM] * 3, flops=10**9, data=3 * 10**6
    )(local, near, far)
    second = lax.all_to_all(p_oth, "lon", 0, 0, tiled=True)

    rows = half_cols // n_lon
    f_own, f_send = call(
        sum_kernel,
        [shape((rows // 2, COLS), f32), shape((rows // 2, COLS), bf16)],
        [VM] * 2,
        [pltpu.VMEM((rows, COLS), f32)],
        flops=10**6,
        data=10**6,
    )(first, second)
    f_oth = lax.ppermute(f_send, "co", swap)
    hr = rows // 2
    (msgs,) = call(
        total_kernel,
        [shape((nz, hr, COLS), bf16)],
        [VM, VM, VM, SM],
        [pltpu.VMEM((2, hr, COLS), f32), pltpu.VMEM((hr, COLS), f32), pltpu.VMEM((2, hr, COLS), f32)],
        flops=10**8,
        data=10**6,
    )(f_own, f_oth, both, ords)

    pack = jnp.concatenate(got, axis=0)
    pack, msgs = lax.optimization_barrier((pack, msgs))
    other_pack = lax.ppermute(pack, "co", swap)
    recv = lax.all_to_all(msgs.reshape(nz * hr, COLS), "z", 0, 0, tiled=True).reshape(nz, hr, COLS)

    def tags_of(p):
        rows_at = [MSG * s + COLS for s in range(3)] + [3 * MSG + COLS // 2]
        return jnp.stack([p[r, :NB] for r in rows_at])

    tags = jnp.stack([tags_of(pack), tags_of(other_pack)]).astype(jnp.int32)
    keep, send = call(
        sweep_kernel,
        [shape((2, hr, COLS), f32), shape((2, hr, COLS), bf16)],
        [VM, ANY, ANY, SM, VM, SM, VM, VM],
        [
            pltpu.VMEM((2, PACK, BLK), bf16),
            pltpu.SemaphoreType.DMA((2,)),
            pltpu.VMEM((2, hr, COLS), f32),
            pltpu.VMEM((2, hr, COLS), f32),
            pltpu.VMEM((2, hr, COLS), f32),
            pltpu.VMEM((2, 2, hr, COLS), f32),
        ],
        flops=10**9,
        data=3 * 10**6,
    )(recv, pack, other_pack, tags, both, ords, f_own, f_oth)
    back = lax.ppermute(send, "co", swap).astype(f32)
    mine_first = jnp.where(co == 0, 1, 0) == 1
    top = jnp.where(mine_first, keep, back)
    bottom = jnp.where(mine_first, back, keep)
    full = jnp.concatenate([top, bottom], axis=1)
    return full[0][None], full[1][None]


def solution(mesh):
    tm, lon, ens = (mesh.shape[a] for a in ("tm", "lon", "ens"))
    fine = Mesh(mesh.devices.reshape(tm // 2, 2, lon, ens), ("z", "co", "lon", "ens"))
    time = ("z", "co")
    placed = (
        P("lon", "ens"),
        P("lon", None, None, None),
        P(time, "lon"),
        P(time, "lon"),
        P(time, None, None, None),
        P(time, None),
    )
    outs = P(time, ("ens", "lon"), None)
    return jax.shard_map(on_device, mesh=fine, in_specs=placed, out_specs=(outs, outs), check_vma=False)
```

```python
import functools

import jax
import jax.numpy as jnp
from jax import lax
from jax.experimental import pallas as pl
from jax.experimental.pallas import tpu as pltpu
from jax.sharding import Mesh
from jax.sharding import PartitionSpec as P

BLK = 128
NB = 8
COLS = NB * BLK
bf16 = jnp.bfloat16
f32 = jnp.float32

VM = pl.BlockSpec(memory_space=pltpu.VMEM)
SM = pl.BlockSpec(memory_space=pltpu.SMEM)
ANY = pl.BlockSpec(memory_space=pl.ANY)

MSG = COLS + 16
HALF = COLS // 2 + 16
MIB = 1024 * 1024


def call(kernel, outs, ins, scratch=(), flops=0, data=0, grant=16, specs=None):
    return pl.pallas_call(
        kernel,
        out_shape=outs,
        in_specs=ins,
        out_specs=specs or [VM] * len(outs),
        scratch_shapes=list(scratch),
        compiler_params=pltpu.CompilerParams(vmem_limit_bytes=grant * MIB),
        cost_estimate=pl.CostEstimate(flops=flops, bytes_accessed=data, transcendentals=0),
    )


def split(x):
    hi = x.astype(bf16)
    lo = (x - hi.astype(f32)).astype(bf16)
    return jnp.concatenate([hi, lo], axis=0)


def cols_at(i):
    return pl.ds(pl.multiple_of(i * BLK, BLK), BLK)


def entry_kernel(innov, cell, anom, tang, order, out, head, tail, msg, innov_v, cell_v, anom_v, tang_v, sem):
    pairs = ((innov, innov_v), (cell, cell_v), (anom, anom_v), (tang, tang_v))
    copies = [pltpu.make_async_copy(a, b, sem.at[i]) for i, (a, b) in enumerate(pairs)]
    for c in copies:
        c.start()
    cells = anom_v.shape[0]
    step = 256
    copies[0].wait()
    copies[1].wait()
    ws = []
    for c in range(0, cells, step):
        ids = lax.broadcasted_iota(jnp.int32, (step, 1), 0) + c
        hit = jnp.where(ids == cell_v[...], innov_v[...], 0.0)
        ws.append(jnp.sum(hit, axis=1, keepdims=True))
    copies[2].wait()
    for j, c in enumerate(range(0, cells, step)):
        y = (ws[j] * anom_v[c : c + step].astype(f32)).astype(bf16)
        out[c : c + step] = y
        if c == 0:
            head[...] = y[:BLK]
        if c + step == cells:
            tail[...] = y[step - BLK :]
    lane = lax.broadcasted_iota(jnp.int32, (16, BLK), 1)
    tag = jnp.zeros((16, BLK), f32)
    for i in range(NB):
        tag = jnp.where(lane == i, order[0, i].astype(f32), tag)
    copies[3].wait()
    msg[:COLS] = tang_v[...].astype(bf16)
    msg[COLS:] = tag.astype(bf16)


def local_kernel(scale, before, mid, after, loc, anom, lout, pout, pad):
    n = mid.shape[0]
    pad[:BLK] = before[...]
    pad[BLK : BLK + n] = mid[...]
    pad[BLK + n :] = after[...]
    for b in range(n // BLK):
        left = jnp.concatenate([loc[b, 0], loc[b, 1], loc[b, 2]], axis=1)
        y = jnp.dot(left, pad[b * BLK : b * BLK + 3 * BLK], preferred_element_type=f32)
        lout[b * BLK : (b + 1) * BLK] = y.astype(bf16)
    y = lax.dot_general(lout[...], anom[...], (((0,), (0,)), ((), ())), preferred_element_type=f32)
    pout[...] = (y * scale).astype(bf16)


def other_kernel(scale, lin, near, far, part, pout):
    co = lax.axis_index("co")
    e = lax.axis_index("ens")
    n = near.shape[0]
    half = part.shape[1]
    dims = (((0,), (0,)), ((), ()))
    mine = lin[pl.ds(pl.multiple_of(co * n, n), n), :]
    rest = lin[pl.ds(pl.multiple_of((1 - co) * n, n), n), :]
    y = lax.dot_general(mine, near[...], dims, preferred_element_type=f32)
    y = y + lax.dot_general(rest, far[...], dims, preferred_element_type=f32)
    pout[:, pl.ds(pl.multiple_of(e * half, half), half)] = part[...]
    pout[:, pl.ds(pl.multiple_of((1 - e) * half, half), half)] = (y * scale).astype(bf16)


def map_kernel(own, oth, ords, both, comp, part):
    co = lax.axis_index("co")
    both[co] = own[:COLS]
    both[1 - co] = oth[:COLS]
    lane = lax.broadcasted_iota(jnp.int32, (16, BLK), 1)
    tag = jnp.zeros((16, BLK), f32)
    for i in range(NB):
        tag = jnp.where(lane == i, ords[0, ords[1, i]].astype(f32), tag)
    ys = []
    for i in range(NB):
        low = both[0, pl.ds(pl.multiple_of(ords[1, i] * BLK, BLK), BLK), :]
        y = jnp.dot(both[1, i * BLK : (i + 1) * BLK], low, preferred_element_type=f32)
        ys.append(y.astype(bf16))
    h = COLS // 2
    for i in range(NB):
        comp[i * BLK : (i + 1) * BLK] = ys[i]
    comp[COLS:] = tag.astype(bf16)
    part[:h] = jnp.where(co == 0, jnp.concatenate(ys[: NB // 2], axis=0), jnp.concatenate(ys[NB // 2 :], axis=0))
    part[h:] = tag.astype(bf16)


def arrange_kernel(mine, theirs, tags, maps, table):
    co = lax.axis_index("co")
    z = lax.axis_index("z")
    nz = maps.shape[0]
    h = COLS // 2

    def fill(low, high, tag_low, tag_high):
        for d in range(1, nz // 2):
            for src, tag, k in ((low, tag_low, z + d), (high, tag_high, z + nz - d)):
                k = lax.rem(k, nz)
                maps[k] = src[(d - 1) * MSG : (d - 1) * MSG + COLS]
                for i in range(NB):
                    table[k, i] = tags[tag, d - 1, i]
        k = lax.rem(z + nz // 2, nz)
        at = (nz // 2 - 1) * MSG
        maps[k, :h] = low[at : at + h]
        maps[k, h:] = high[at : at + h]
        for i in range(NB):
            table[k, i] = tags[0, nz // 2 - 1, i]
            table[z, i] = 0

    @pl.when(co == 0)
    def _():
        fill(mine, theirs, 0, 1)

    @pl.when(co == 1)
    def _():
        fill(theirs, mine, 1, 0)


def sum_kernel(parts, own, send):
    co = lax.axis_index("co")
    n, rows, _ = parts.shape
    h = rows // 2
    for place, out in ((co, own), (1 - co, send)):
        at = pl.ds(pl.multiple_of(place * h, h), h)
        y = parts[0, at, :].astype(f32)
        for s in range(1, n):
            y = y + parts[s, at, :].astype(f32)
        out[...] = y.astype(out.dtype)


def apply_forward(src, blocks, order, add):
    xs = [split(src[:, cols_at(order(i))]) for i in range(NB)]
    ys = []
    for i in range(NB):
        y = lax.dot_general(xs[i], blocks(i), (((1,), (1,)), ((), ())), preferred_element_type=f32)
        h = y.shape[0] // 2
        ys.append(y[:h] + y[h:] + add(i))
    return ys


def apply_adjoint(xs, blocks):
    ys = []
    for i in range(NB):
        y = lax.dot_general(split(xs[i]), blocks(i), (((1,), (0,)), ((), ())), preferred_element_type=f32)
        h = y.shape[0] // 2
        ys.append(y[:h] + y[h:])
    return ys


def cut(x, i):
    return x[:, i * BLK : (i + 1) * BLK]


def block_of(both, t):
    return lambda i: both[t, i * BLK : (i + 1) * BLK]


def total_kernel(own, oth, both, ords, out, low, tot, tmp):
    co = lax.axis_index("co")
    z = lax.axis_index("z")
    mine = own[...]
    other = oth[...].astype(f32)
    first = jnp.where(co == 0, mine, other)
    second = jnp.where(co == 0, other, mine)
    low[...] = first
    ys = apply_adjoint([cut(second, i) for i in range(NB)], block_of(both, 1))
    fs = apply_forward(low, block_of(both, 1), lambda i: ords[1, i], lambda i: cut(second, i))
    for i in range(NB):
        tmp[:, cols_at(ords[1, i])] = ys[i]
    back = tmp[...] + first
    ys = apply_adjoint([cut(back, i) for i in range(NB)], block_of(both, 0))
    for i in range(NB):
        tot[:, cols_at(ords[0, i])] = ys[i].astype(bf16)
    adj = tot[...]
    fwd = jnp.concatenate(fs, axis=1).astype(bf16)
    for d in range(out.shape[0]):
        out[d] = jnp.where(d > z, fwd, adj)


def sweep_kernel(recv, maps, tags, both, ords, own, oth, keep, send, st, adj, res):
    co = lax.axis_index("co")
    z = lax.axis_index("z")
    nz = recv.shape[0]
    mine = own[...]
    other = oth[...].astype(f32)
    force = (jnp.where(co == 0, mine, other), jnp.where(co == 0, other, mine))
    st[...] = jnp.where(z > 0, recv[0].astype(f32), 0.0)
    adj[...] = jnp.where(z < nz - 1, recv[nz - 1].astype(f32), 0.0)

    def block(k):
        return lambda i: maps[k, i * BLK : (i + 1) * BLK]

    def forward(k, carry):
        ys = apply_forward(
            st, block(k), lambda i: tags[k, i], lambda i: recv[k, :, i * BLK : (i + 1) * BLK].astype(f32)
        )
        for i in range(NB):
            st[:, i * BLK : (i + 1) * BLK] = ys[i]
        return carry

    def backward(s, carry):
        k = nz - 1 - s
        ys = apply_adjoint([adj[:, i * BLK : (i + 1) * BLK] for i in range(NB)], block(k))
        more = [recv[k, :, cols_at(tags[k, i])].astype(f32) for i in range(NB)]
        for i in range(NB):
            adj[:, cols_at(tags[k, i])] = ys[i] + more[i]
        return carry

    lax.fori_loop(1, z, forward, 0)
    lax.fori_loop(1, nz - 1 - z, backward, 0)
    up = adj[...] + force[1]
    x0 = apply_forward(st, block_of(both, 0), lambda i: ords[0, i], lambda i: cut(force[0], i))
    y1 = apply_adjoint([cut(up, i) for i in range(NB)], block_of(both, 1))
    for i in range(NB):
        res[0, 0, :, i * BLK : (i + 1) * BLK] = x0[i]
    for i in range(NB):
        res[1, 1, :, cols_at(ords[1, i])] = y1[i]
    up = res[1, 1] + force[0]
    x1 = apply_forward(res.at[0, 0], block_of(both, 1), lambda i: ords[1, i], lambda i: cut(force[1], i))
    y0 = apply_adjoint([cut(up, i) for i in range(NB)], block_of(both, 0))
    for i in range(NB):
        res[1, 0, :, i * BLK : (i + 1) * BLK] = x1[i]
    for i in range(NB):
        res[0, 1, :, cols_at(ords[0, i])] = y0[i]
    keep[...] = res[co]
    send[...] = res[1 - co].astype(bf16)


def join_kernel(keep, back, x, y):
    co = lax.axis_index("co")
    h = keep.shape[1]
    for j, out in enumerate((x, y)):
        out[0, pl.ds(pl.multiple_of(co * h, h), h), :] = keep[j]
        out[0, pl.ds(pl.multiple_of((1 - co) * h, h), h), :] = back[j].astype(f32)


def on_device(anomalies, localization, innovations, obs_cell, tangent_blocks, tangent_order):
    cells, half_cols = anomalies.shape
    n_lon = lax.axis_size("lon")
    nz = lax.axis_size("z")
    co = lax.axis_index("co")
    shape = jax.ShapeDtypeStruct
    swap = [(0, 1), (1, 0)]
    scale = float(cells * n_lon) ** (-0.5)

    h = cells // 2
    piece = lax.dynamic_slice_in_dim(anomalies, co * h, h, 0)
    near = lax.ppermute(piece, "ens", swap)

    weighted, head, tail, own_map = call(
        entry_kernel,
        [
            shape((cells, half_cols), bf16),
            shape((BLK, half_cols), bf16),
            shape((BLK, half_cols), bf16),
            shape((MSG, BLK), bf16),
        ],
        [ANY] * 4 + [SM],
        [
            pltpu.VMEM(innovations.shape, f32),
            pltpu.VMEM(obs_cell.shape, jnp.int32),
            pltpu.VMEM(anomalies.shape, bf16),
            pltpu.VMEM((COLS, BLK), f32),
            pltpu.SemaphoreType.DMA((4,)),
        ],
        flops=10**6,
        data=2 * 10**6,
    )(innovations, obs_cell, anomalies, tangent_blocks.reshape(COLS, BLK), tangent_order)
    up = [(i, (i + 1) % n_lon) for i in range(n_lon)]
    down = [(b, a) for a, b in up]
    before = lax.ppermute(tail, "lon", up)
    after = lax.ppermute(head, "lon", down)
    oth_map = lax.ppermute(own_map, "co", swap)

    order_own = tangent_order[0]
    order_oth = oth_map[COLS, :NB].astype(jnp.int32)
    ords = jnp.where(co == 0, jnp.stack([order_own, order_oth]), jnp.stack([order_oth, order_own]))
    both, comp, part = call(
        map_kernel,
        [shape((2, COLS, BLK), bf16), shape((MSG, BLK), bf16), shape((HALF, BLK), bf16)],
        [VM, VM, SM],
        flops=10**7,
        data=2 * 10**6,
    )(own_map, oth_map, ords)
    got = []
    for d in range(1, nz // 2):
        pairs = []
        for k in range(nz):
            pairs.append((((k + d) % nz) * 2, k * 2))
            pairs.append((((k - d) % nz) * 2 + 1, k * 2 + 1))
        got.append(lax.ppermute(comp, ("z", "co"), pairs))
    got.append(lax.ppermute(part, "z", [((k + nz // 2) % nz, k) for k in range(nz)]))

    local, p_own = call(
        functools.partial(local_kernel, scale),
        [shape((cells, half_cols), bf16), shape((half_cols, half_cols), bf16)],
        [VM] * 5,
        [pltpu.VMEM((cells + 2 * BLK, half_cols), bf16)],
        flops=10**9,
        data=4 * 10**6,
    )(before, weighted, after, localization, anomalies)
    far = lax.ppermute(near, "co", swap)
    (p_all,) = call(
        functools.partial(other_kernel, scale), [shape((half_cols, COLS), bf16)], [VM] * 4, flops=10**9, data=3 * 10**6
    )(local, near, far, p_own)
    rows = half_cols // n_lon
    parts = lax.all_to_all(p_all, "lon", 0, 0, tiled=True).reshape(n_lon, rows, COLS)

    hr = rows // 2
    f_own, f_send = call(
        sum_kernel, [shape((hr, COLS), f32), shape((hr, COLS), bf16)], [VM], flops=10**6, data=10**6
    )(parts)
    f_oth = lax.ppermute(f_send, "co", swap)
    (msgs,) = call(
        total_kernel,
        [shape((nz, hr, COLS), bf16)],
        [VM, VM, VM, SM],
        [pltpu.VMEM((hr, COLS), f32), pltpu.VMEM((hr, COLS), bf16), pltpu.VMEM((hr, COLS), f32)],
        flops=10**8,
        data=10**6,
    )(f_own, f_oth, both, ords)
    recv = lax.all_to_all(msgs, "z", 0, 0, tiled=True)

    near_maps = jnp.concatenate(got, axis=0)
    near_maps, msgs = lax.optimization_barrier((near_maps, msgs))
    far_maps = lax.ppermute(near_maps, "co", swap)
    starts = [MSG * j + COLS for j in range(nz // 2 - 1)] + [MSG * (nz // 2 - 1) + COLS // 2]
    tags = jnp.stack([jnp.stack([p[r, :NB] for r in starts]) for p in (near_maps, far_maps)]).astype(jnp.int32)
    maps, table = call(
        arrange_kernel,
        [shape((nz, COLS, BLK), bf16), shape((nz, NB), jnp.int32)],
        [VM, VM, SM],
        flops=10**6,
        data=4 * 10**6,
        specs=[VM, SM],
    )(near_maps, far_maps, tags)
    keep, send = call(
        sweep_kernel,
        [shape((2, hr, COLS), f32), shape((2, hr, COLS), bf16)],
        [VM, VM, SM, VM, SM, VM, VM],
        [
            pltpu.VMEM((hr, COLS), f32),
            pltpu.VMEM((hr, COLS), f32),
            pltpu.VMEM((2, 2, hr, COLS), f32),
        ],
        flops=10**9,
        data=3 * 10**6,
    )(recv, maps, table, both, ords, f_own, f_oth)
    back = lax.ppermute(send, "co", swap)
    x, y = call(join_kernel, [shape((1, rows, COLS), f32)] * 2, [VM] * 2, flops=10**6, data=10**6)(keep, back)
    return x, y


def solution(mesh):
    tm, lon, ens = (mesh.shape[a] for a in ("tm", "lon", "ens"))
    fine = Mesh(mesh.devices.reshape(tm // 2, 2, lon, ens), ("z", "co", "lon", "ens"))
    time = ("z", "co")
    placed = (
        P("lon", "ens"),
        P("lon", None, None, None),
        P(time, "lon"),
        P(time, "lon"),
        P(time, None, None, None),
        P(time, None),
    )
    outs = P(time, ("ens", "lon"), None)

    return jax.shard_map(on_device, mesh=fine, in_specs=placed, out_specs=(outs, outs), check_vma=False)
```

```python
import functools

import jax
import jax.numpy as jnp
from jax import lax
from jax.experimental import pallas as pl
from jax.experimental.pallas import tpu as pltpu
from jax.sharding import Mesh
from jax.sharding import PartitionSpec as P

BLK = 128
NB = 8
COLS = NB * BLK
bf16 = jnp.bfloat16
f32 = jnp.float32

VM = pl.BlockSpec(memory_space=pltpu.VMEM)
SM = pl.BlockSpec(memory_space=pltpu.SMEM)
HBM = pl.BlockSpec(memory_space=pltpu.HBM)

MSG = COLS + 16
MIB = 1024 * 1024


def call(kernel, outs, ins, scratch=(), flops=0, data=0, grant=16, specs=None):
    made = pl.pallas_call(
        kernel,
        out_shape=outs,
        in_specs=ins,
        out_specs=specs or [VM] * len(outs),
        scratch_shapes=list(scratch),
        compiler_params=pltpu.CompilerParams(vmem_limit_bytes=grant * MIB),
        cost_estimate=pl.CostEstimate(flops=flops, bytes_accessed=data, transcendentals=0),
    )

    def run(*args):
        args = [pltpu.with_memory_space_constraint(a, pltpu.HBM) if i is HBM else a for a, i in zip(args, ins)]
        return made(*args)

    return run


def split(x):
    hi = x.astype(bf16)
    lo = (x - hi.astype(f32)).astype(bf16)
    return jnp.concatenate([hi, lo], axis=0)


def cols_at(i):
    return pl.ds(pl.multiple_of(i * BLK, BLK), BLK)


def weights(cell, innov, start, count):
    ids = lax.broadcasted_iota(jnp.int32, (count, 1), 0) + start
    return jnp.sum(jnp.where(ids == cell[...], innov[...], 0.0), axis=1, keepdims=True)


def entry_kernel(innov, cell, anom, tang, order, head, tail, piece, msg, innov_v, cell_v, edge, tang_v, order_s, sem):
    co = lax.axis_index("co")
    cells = anom.shape[0]
    h = piece.shape[0]
    pairs = (
        (innov, innov_v),
        (cell, cell_v),
        (anom.at[pl.ds(0, BLK)], edge.at[0]),
        (anom.at[pl.ds(cells - BLK, BLK)], edge.at[1]),
        (tang, tang_v),
        (anom.at[pl.ds(pl.multiple_of(co * h, h), h)], piece),
        (order, order_s),
    )
    copies = [pltpu.make_async_copy(a, b, sem.at[i]) for i, (a, b) in enumerate(pairs)]
    for c in copies:
        c.start()
    copies[0].wait()
    copies[1].wait()
    w0 = weights(cell_v, innov_v, 0, BLK)
    w1 = weights(cell_v, innov_v, cells - BLK, BLK)
    copies[2].wait()
    copies[3].wait()
    head[...] = (w0 * edge[0].astype(f32)).astype(bf16)
    tail[...] = (w1 * edge[1].astype(f32)).astype(bf16)
    copies[6].wait()
    lane = lax.broadcasted_iota(jnp.int32, (16, BLK), 1)
    tag = jnp.zeros((16, BLK), f32)
    for i in range(NB):
        tag = jnp.where(lane == i, order_s[0, i].astype(f32), tag)
    msg[COLS:] = tag.astype(bf16)
    copies[4].wait()
    msg[:COLS] = tang_v[...].astype(bf16)
    copies[5].wait()


def inner_kernel(innov, cell, anom, loc, out, anom_v, loc_v, innov_v, cell_v, sem):
    pairs = ((innov, innov_v), (cell, cell_v), (anom, anom_v), (loc, loc_v))
    copies = [pltpu.make_async_copy(a, b, sem.at[i]) for i, (a, b) in enumerate(pairs)]
    for c in copies:
        c.start()
    copies[0].wait()
    copies[1].wait()
    cells = out.shape[0]
    step = 256
    ws = [weights(cell_v, innov_v, c, step) for c in range(0, cells, step)]
    copies[2].wait()
    for j, c in enumerate(range(0, cells, step)):
        out[c : c + step] = (ws[j] * anom_v[c : c + step].astype(f32)).astype(bf16)
    copies[3].wait()


def local_kernel(scale, before, mid, after, loc, anom, lout, pout):
    n = mid.shape[0] // BLK
    for b in range(n):
        left = jnp.concatenate([loc[b, 0], loc[b, 1], loc[b, 2]], axis=1)
        if b == 0:
            right = jnp.concatenate([before[...], mid[: 2 * BLK]], axis=0)
        elif b == n - 1:
            right = jnp.concatenate([mid[(b - 1) * BLK :], after[...]], axis=0)
        else:
            right = mid[(b - 1) * BLK : (b + 2) * BLK]
        y = jnp.dot(left, right, preferred_element_type=f32)
        lout[b * BLK : (b + 1) * BLK] = y.astype(bf16)
    y = lax.dot_general(lout[...], anom[...], (((0,), (0,)), ((), ())), preferred_element_type=f32)
    pout[...] = (y * scale).astype(bf16)


def other_kernel(scale, lin, near, far, part, pout):
    co = lax.axis_index("co")
    e = lax.axis_index("ens")
    n = near.shape[0]
    half = part.shape[1]
    dims = (((0,), (0,)), ((), ()))
    mine = lin[pl.ds(pl.multiple_of(co * n, n), n), :]
    rest = lin[pl.ds(pl.multiple_of((1 - co) * n, n), n), :]
    y = lax.dot_general(mine, near[...], dims, preferred_element_type=f32)
    y = y + lax.dot_general(rest, far[...], dims, preferred_element_type=f32)
    pout[:, pl.ds(pl.multiple_of(e * half, half), half)] = part[...]
    pout[:, pl.ds(pl.multiple_of((1 - e) * half, half), half)] = (y * scale).astype(bf16)


def map_kernel(own, oth, both, comp, ords, ints, sem):
    co = lax.axis_index("co")
    both[co] = own[:COLS]
    both[1 - co] = oth[:COLS]
    mine = own[COLS:].astype(f32)[:8].astype(jnp.int32)
    other = oth[COLS:].astype(f32)[:8].astype(jnp.int32)
    row = lax.broadcasted_iota(jnp.int32, (8, BLK), 0)
    ints[...] = jnp.where(row == co, mine, other)
    c = pltpu.make_async_copy(ints, ords, sem)
    c.start()
    c.wait()
    lane = lax.broadcasted_iota(jnp.int32, (16, BLK), 1)
    tag = jnp.zeros((16, BLK), f32)
    for i in range(NB):
        tag = jnp.where(lane == i, ords[0, ords[1, i]].astype(f32), tag)
    for i in range(NB):
        low = both[0, pl.ds(pl.multiple_of(ords[1, i] * BLK, BLK), BLK), :]
        y = jnp.dot(both[1, i * BLK : (i + 1) * BLK], low, preferred_element_type=f32)
        comp[i * BLK : (i + 1) * BLK] = y.astype(bf16)
    comp[COLS:] = tag.astype(bf16)


def arrange_kernel(*refs):
    *got, maps, table, ints, sem = refs
    co = lax.axis_index("co")
    z = lax.axis_index("z")
    nz = maps.shape[0]
    for j, src in enumerate(got):
        d = j + 1 if j < nz // 2 else j + 1 - nz // 2
        back = co == 0 if j < nz // 2 else co == 1
        k = lax.rem(jnp.where(back, z + nz - d, z + d), nz)
        maps[k] = src[:COLS]
        ints[pl.ds(k, 1), :] = src[COLS:].astype(f32)[:1].astype(jnp.int32)
    ints[pl.ds(z, 1), :] = jnp.zeros((1, BLK), jnp.int32)
    c = pltpu.make_async_copy(ints, table, sem)
    c.start()
    c.wait()


def sum_kernel(parts, own, send):
    co = lax.axis_index("co")
    n, rows, _ = parts.shape
    h = rows // 2
    for place, out in ((co, own), (1 - co, send)):
        at = pl.ds(pl.multiple_of(place * h, h), h)
        y = parts[0, at, :].astype(f32)
        for s in range(1, n):
            y = y + parts[s, at, :].astype(f32)
        out[...] = y.astype(out.dtype)


def apply_forward(src, blocks, order, add):
    xs = [split(src[:, cols_at(order(i))]) for i in range(NB)]
    ys = []
    for i in range(NB):
        y = lax.dot_general(xs[i], blocks(i), (((1,), (1,)), ((), ())), preferred_element_type=f32)
        h = y.shape[0] // 2
        ys.append(y[:h] + y[h:] + add(i))
    return ys


def apply_adjoint(xs, blocks):
    ys = []
    for i in range(NB):
        y = lax.dot_general(split(xs[i]), blocks(i), (((1,), (0,)), ((), ())), preferred_element_type=f32)
        h = y.shape[0] // 2
        ys.append(y[:h] + y[h:])
    return ys


def cut(x, i):
    return x[:, i * BLK : (i + 1) * BLK]


def block_of(both, t):
    return lambda i: both[t, i * BLK : (i + 1) * BLK]


def total_kernel(own, oth, both, ords, out, low, tot, tmp):
    co = lax.axis_index("co")
    z = lax.axis_index("z")
    mine = own[...]
    other = oth[...].astype(f32)
    first = jnp.where(co == 0, mine, other)
    second = jnp.where(co == 0, other, mine)
    low[...] = first
    ys = apply_adjoint([cut(second, i) for i in range(NB)], block_of(both, 1))
    fs = apply_forward(low, block_of(both, 1), lambda i: ords[1, i], lambda i: cut(second, i))
    for i in range(NB):
        tmp[:, cols_at(ords[1, i])] = ys[i]
    back = tmp[...] + first
    ys = apply_adjoint([cut(back, i) for i in range(NB)], block_of(both, 0))
    for i in range(NB):
        tot[:, cols_at(ords[0, i])] = ys[i].astype(bf16)
    adj = tot[...]
    fwd = jnp.concatenate(fs, axis=1).astype(bf16)
    for d in range(out.shape[0]):
        out[d] = jnp.where(d > z, fwd, adj)


def sweep_kernel(recv, stored, tags, both, ords, own, oth, keep, send, maps, st, adj, res, sem):
    co = lax.axis_index("co")
    z = lax.axis_index("z")
    nz = recv.shape[0]

    def copy(k):
        return pltpu.make_async_copy(stored.at[k], maps.at[k], sem.at[k])

    for j in range(1, nz // 2):
        for k in (j, nz - 1 - j):

            @pl.when(k != z)
            def _():
                copy(k).start()

    mine = own[...]
    other = oth[...].astype(f32)
    force = (jnp.where(co == 0, mine, other), jnp.where(co == 0, other, mine))
    st[...] = jnp.where(z > 0, recv[0].astype(f32), 0.0)
    adj[...] = jnp.where(z < nz - 1, recv[nz - 1].astype(f32), 0.0)

    def block(k):
        return lambda i: maps[k, i * BLK : (i + 1) * BLK]

    def forward(k, carry):
        copy(k).wait()
        ys = apply_forward(
            st, block(k), lambda i: tags[k, i], lambda i: recv[k, :, i * BLK : (i + 1) * BLK].astype(f32)
        )
        for i in range(NB):
            st[:, i * BLK : (i + 1) * BLK] = ys[i]
        return carry

    def backward(s, carry):
        k = nz - 1 - s
        copy(k).wait()
        ys = apply_adjoint([adj[:, i * BLK : (i + 1) * BLK] for i in range(NB)], block(k))
        more = [recv[k, :, cols_at(tags[k, i])].astype(f32) for i in range(NB)]
        for i in range(NB):
            adj[:, cols_at(tags[k, i])] = ys[i] + more[i]
        return carry

    lax.fori_loop(1, z, forward, 0)
    lax.fori_loop(1, nz - 1 - z, backward, 0)
    up = adj[...] + force[1]
    x0 = apply_forward(st, block_of(both, 0), lambda i: ords[0, i], lambda i: cut(force[0], i))
    y1 = apply_adjoint([cut(up, i) for i in range(NB)], block_of(both, 1))
    for i in range(NB):
        res[0, 0, :, i * BLK : (i + 1) * BLK] = x0[i]
    for i in range(NB):
        res[1, 1, :, cols_at(ords[1, i])] = y1[i]
    up = res[1, 1] + force[0]
    x1 = apply_forward(res.at[0, 0], block_of(both, 1), lambda i: ords[1, i], lambda i: cut(force[1], i))
    y0 = apply_adjoint([cut(up, i) for i in range(NB)], block_of(both, 0))
    for i in range(NB):
        res[1, 0, :, i * BLK : (i + 1) * BLK] = x1[i]
    for i in range(NB):
        res[0, 1, :, cols_at(ords[0, i])] = y0[i]
    keep[...] = res[co]
    send[...] = res[1 - co].astype(bf16)


def join_kernel(keep, back, x, y):
    co = lax.axis_index("co")
    h = keep.shape[1]
    for j, out in enumerate((x, y)):
        out[0, pl.ds(pl.multiple_of(co * h, h), h), :] = keep[j]
        out[0, pl.ds(pl.multiple_of((1 - co) * h, h), h), :] = back[j].astype(f32)


def on_device(anomalies, localization, innovations, obs_cell, tangent_blocks, tangent_order):
    cells, half_cols = anomalies.shape
    n_lon = lax.axis_size("lon")
    nz = lax.axis_size("z")
    shape = jax.ShapeDtypeStruct
    swap = [(0, 1), (1, 0)]
    scale = float(cells * n_lon) ** (-0.5)

    head, tail, piece, own_map = call(
        entry_kernel,
        [
            shape((BLK, half_cols), bf16),
            shape((BLK, half_cols), bf16),
            shape((cells // 2, half_cols), bf16),
            shape((MSG, BLK), bf16),
        ],
        [HBM] * 5,
        [
            pltpu.VMEM(innovations.shape, f32),
            pltpu.VMEM(obs_cell.shape, jnp.int32),
            pltpu.VMEM((2, BLK, half_cols), bf16),
            pltpu.VMEM((COLS, BLK), f32),
            pltpu.SMEM(tangent_order.shape, jnp.int32),
            pltpu.SemaphoreType.DMA((7,)),
        ],
        flops=10**6,
        data=2 * 10**6,
    )(innovations, obs_cell, anomalies, tangent_blocks.reshape(COLS, BLK), tangent_order)
    up = [(i, (i + 1) % n_lon) for i in range(n_lon)]
    down = [(b, a) for a, b in up]
    near = lax.ppermute(piece, "ens", swap)
    before = lax.ppermute(tail, "lon", up)
    after = lax.ppermute(head, "lon", down)
    oth_map = lax.ppermute(own_map, "co", swap)

    both, comp, ords = call(
        map_kernel,
        [shape((2, COLS, BLK), bf16), shape((MSG, BLK), bf16), shape((8, BLK), jnp.int32)],
        [VM, VM],
        [pltpu.VMEM((8, BLK), jnp.int32), pltpu.SemaphoreType.DMA],
        flops=10**7,
        data=2 * 10**6,
        specs=[VM, VM, SM],
    )(own_map, oth_map)
    around = []
    for k in range(nz):
        around.append((k * 2, (k + 1) % nz * 2))
        around.append(((k + 1) % nz * 2 + 1, k * 2 + 1))
    got = []
    held = comp
    for _ in range(1, nz // 2 + 1):
        held = lax.ppermute(held, ("z", "co"), around)
        got.append(held)

    weighted, anom_v, loc_v = call(
        inner_kernel,
        [shape((cells, half_cols), bf16), shape(anomalies.shape, bf16), shape(localization.shape, bf16)],
        [HBM] * 4,
        [pltpu.VMEM(innovations.shape, f32), pltpu.VMEM(obs_cell.shape, jnp.int32), pltpu.SemaphoreType.DMA((4,))],
        flops=10**6,
        data=4 * 10**6,
    )(innovations, obs_cell, anomalies, localization)
    local, p_own = call(
        functools.partial(local_kernel, scale),
        [shape((cells, half_cols), bf16), shape((half_cols, half_cols), bf16)],
        [VM] * 5,
        flops=10**9,
        data=4 * 10**6,
    )(before, weighted, after, loc_v, anom_v)
    far = lax.ppermute(near, "co", swap)
    (p_all,) = call(
        functools.partial(other_kernel, scale), [shape((half_cols, COLS), bf16)], [VM] * 4, flops=10**9, data=3 * 10**6
    )(local, near, far, p_own)
    rows = half_cols // n_lon
    parts = lax.all_to_all(p_all, "lon", 0, 0, tiled=True).reshape(n_lon, rows, COLS)

    hr = rows // 2
    f_own, f_send = call(
        sum_kernel, [shape((hr, COLS), f32), shape((hr, COLS), bf16)], [VM], flops=10**6, data=10**6
    )(parts)
    f_oth = lax.ppermute(f_send, "co", swap)
    (msgs,) = call(
        total_kernel,
        [shape((nz, hr, COLS), bf16)],
        [VM, VM, VM, SM],
        [pltpu.VMEM((hr, COLS), f32), pltpu.VMEM((hr, COLS), bf16), pltpu.VMEM((hr, COLS), f32)],
        flops=10**8,
        data=10**6,
    )(f_own, f_oth, both, ords)
    recv = lax.all_to_all(msgs, "z", 0, 0, tiled=True)

    tied = lax.optimization_barrier((msgs, *got))
    got = list(tied[1:])
    for j in range(nz // 2 - 1):
        got.append(lax.ppermute(got[j], "co", swap))
    maps, table = call(
        arrange_kernel,
        [shape((nz, COLS, BLK), bf16), shape((nz, BLK), jnp.int32)],
        [VM] * len(got),
        [pltpu.VMEM((nz, BLK), jnp.int32), pltpu.SemaphoreType.DMA],
        flops=10**6,
        data=4 * 10**6,
        specs=[VM, SM],
    )(*got)
    keep, send = call(
        sweep_kernel,
        [shape((2, hr, COLS), f32), shape((2, hr, COLS), bf16)],
        [VM, HBM, SM, VM, SM, VM, VM],
        [
            pltpu.VMEM((nz, COLS, BLK), bf16),
            pltpu.VMEM((hr, COLS), f32),
            pltpu.VMEM((hr, COLS), f32),
            pltpu.VMEM((2, 2, hr, COLS), f32),
            pltpu.SemaphoreType.DMA((nz,)),
        ],
        flops=10**9,
        data=3 * 10**6,
    )(recv, maps, table, both, ords, f_own, f_oth)
    back = lax.ppermute(send, "co", swap)
    x, y = call(join_kernel, [shape((1, rows, COLS), f32)] * 2, [VM] * 2, flops=10**6, data=10**6)(keep, back)
    return x, y


def solution(mesh):
    tm, lon, ens = (mesh.shape[a] for a in ("tm", "lon", "ens"))
    fine = Mesh(mesh.devices.reshape(tm // 2, 2, lon, ens), ("z", "co", "lon", "ens"))
    time = ("z", "co")
    placed = (
        P("lon", "ens"),
        P("lon", None, None, None),
        P(time, "lon"),
        P(time, "lon"),
        P(time, None, None, None),
        P(time, None),
    )
    outs = P(time, ("ens", "lon"), None)

    return jax.shard_map(on_device, mesh=fine, in_specs=placed, out_specs=(outs, outs), check_vma=False)
```

```python
import functools

import jax
import jax.numpy as jnp
from jax import lax
from jax.experimental import pallas as pl
from jax.experimental.pallas import tpu as pltpu
from jax.sharding import Mesh
from jax.sharding import PartitionSpec as P

BLK = 128
NB = 8
COLS = NB * BLK
bf16 = jnp.bfloat16
f32 = jnp.float32

VM = pl.BlockSpec(memory_space=pltpu.VMEM)
SM = pl.BlockSpec(memory_space=pltpu.SMEM)
HBM = pl.BlockSpec(memory_space=pltpu.HBM)

MSG = COLS + 16
MIB = 1024 * 1024


def call(kernel, outs, ins, scratch=(), flops=0, data=0, grant=16, specs=None):
    made = pl.pallas_call(
        kernel,
        out_shape=outs,
        in_specs=ins,
        out_specs=specs or [VM] * len(outs),
        scratch_shapes=list(scratch),
        compiler_params=pltpu.CompilerParams(vmem_limit_bytes=grant * MIB),
        cost_estimate=pl.CostEstimate(flops=flops, bytes_accessed=data, transcendentals=0),
    )

    def run(*args):
        args = [pltpu.with_memory_space_constraint(a, pltpu.HBM) if i is HBM else a for a, i in zip(args, ins)]
        return made(*args)

    return run


def split(x):
    hi = x.astype(bf16)
    lo = (x - hi.astype(f32)).astype(bf16)
    return jnp.concatenate([hi, lo], axis=0)


def cols_at(i):
    return pl.ds(pl.multiple_of(i * BLK, BLK), BLK)


def weights(cell, innov, start, count):
    ids = lax.broadcasted_iota(jnp.int32, (count, 1), 0) + start
    return jnp.sum(jnp.where(ids == cell[...], innov[...], 0.0), axis=1, keepdims=True)


def entry_kernel(innov, cell, anom, tang, order, head, tail, msg, innov_v, cell_v, edge, tang_v, order_s, sem):
    cells = anom.shape[0]
    pairs = (
        (innov, innov_v),
        (cell, cell_v),
        (anom.at[pl.ds(0, BLK)], edge.at[0]),
        (anom.at[pl.ds(cells - BLK, BLK)], edge.at[1]),
        (tang, tang_v),
        (order, order_s),
    )
    copies = [pltpu.make_async_copy(a, b, sem.at[i]) for i, (a, b) in enumerate(pairs)]
    for c in copies:
        c.start()
    copies[0].wait()
    copies[1].wait()
    w0 = weights(cell_v, innov_v, 0, BLK)
    w1 = weights(cell_v, innov_v, cells - BLK, BLK)
    copies[2].wait()
    copies[3].wait()
    head[...] = (w0 * edge[0].astype(f32)).astype(bf16)
    tail[...] = (w1 * edge[1].astype(f32)).astype(bf16)
    copies[5].wait()
    lane = lax.broadcasted_iota(jnp.int32, (16, BLK), 1)
    tag = jnp.zeros((16, BLK), f32)
    for i in range(NB):
        tag = jnp.where(lane == i, order_s[0, i].astype(f32), tag)
    msg[COLS:] = tag.astype(bf16)
    copies[4].wait()
    msg[:COLS] = tang_v[...].astype(bf16)


def inner_kernel(innov, cell, anom, loc, out, anom_v, loc_v, innov_v, cell_v, sem):
    pairs = ((innov, innov_v), (cell, cell_v), (anom, anom_v), (loc, loc_v))
    copies = [pltpu.make_async_copy(a, b, sem.at[i]) for i, (a, b) in enumerate(pairs)]
    for c in copies:
        c.start()
    copies[0].wait()
    copies[1].wait()
    cells = out.shape[0]
    step = 256
    ws = [weights(cell_v, innov_v, c, step) for c in range(0, cells, step)]
    copies[2].wait()
    for j, c in enumerate(range(0, cells, step)):
        out[c : c + step] = (ws[j] * anom_v[c : c + step].astype(f32)).astype(bf16)
    copies[3].wait()


def local_kernel(before, mid, after, loc, lout):
    n = mid.shape[0] // BLK
    for b in range(n):
        left = jnp.concatenate([loc[b, 0], loc[b, 1], loc[b, 2]], axis=1)
        if b == 0:
            right = jnp.concatenate([before[...], mid[: 2 * BLK]], axis=0)
        elif b == n - 1:
            right = jnp.concatenate([mid[(b - 1) * BLK :], after[...]], axis=0)
        else:
            right = mid[(b - 1) * BLK : (b + 2) * BLK]
        y = jnp.dot(left, right, preferred_element_type=f32)
        lout[b * BLK : (b + 1) * BLK] = y.astype(bf16)


def product_kernel(scale, mine, theirs, anom, fetched, pout):
    co = lax.axis_index("co")
    half = anom.shape[1]
    dims = (((0,), (0,)), ((), ()))

    def fill(right):
        for src, t in ((mine, co), (theirs, 1 - co)):
            y = lax.dot_general(src[...], right[...], dims, preferred_element_type=f32)
            pout[:, pl.ds(pl.multiple_of(t * half, half), half)] = (y * scale).astype(bf16)

    own = co == lax.axis_index("ens")

    @pl.when(own)
    def _():
        fill(anom)

    @pl.when(jnp.logical_not(own))
    def _():
        fill(fetched)


def map_kernel(own, oth, both, comp, ords, ints, sem):
    co = lax.axis_index("co")
    both[co] = own[:COLS]
    both[1 - co] = oth[:COLS]
    mine = own[COLS:].astype(f32)[:8].astype(jnp.int32)
    other = oth[COLS:].astype(f32)[:8].astype(jnp.int32)
    row = lax.broadcasted_iota(jnp.int32, (8, BLK), 0)
    ints[...] = jnp.where(row == co, mine, other)
    c = pltpu.make_async_copy(ints, ords, sem)
    c.start()
    c.wait()
    lane = lax.broadcasted_iota(jnp.int32, (16, BLK), 1)
    tag = jnp.zeros((16, BLK), f32)
    for i in range(NB):
        tag = jnp.where(lane == i, ords[0, ords[1, i]].astype(f32), tag)
    for i in range(NB):
        low = both[0, pl.ds(pl.multiple_of(ords[1, i] * BLK, BLK), BLK), :]
        y = jnp.dot(both[1, i * BLK : (i + 1) * BLK], low, preferred_element_type=f32)
        comp[i * BLK : (i + 1) * BLK] = y.astype(bf16)
    comp[COLS:] = tag.astype(bf16)


def arrange_kernel(*refs):
    *got, maps, table, ints, sem = refs
    co = lax.axis_index("co")
    z = lax.axis_index("z")
    nz = maps.shape[0]
    for j, src in enumerate(got):
        d = j + 1 if j < nz // 2 else j + 1 - nz // 2
        back = co == 0 if j < nz // 2 else co == 1
        k = lax.rem(jnp.where(back, z + nz - d, z + d), nz)
        maps[k] = src[:COLS]
        ints[pl.ds(k, 1), :] = src[COLS:].astype(f32)[:1].astype(jnp.int32)
    ints[pl.ds(z, 1), :] = jnp.zeros((1, BLK), jnp.int32)
    c = pltpu.make_async_copy(ints, table, sem)
    c.start()
    c.wait()


def sum_kernel(parts, own, send):
    co = lax.axis_index("co")
    n, rows, _ = parts.shape
    h = rows // 2
    for place, out in ((co, own), (1 - co, send)):
        at = pl.ds(pl.multiple_of(place * h, h), h)
        y = parts[0, at, :].astype(f32)
        for s in range(1, n):
            y = y + parts[s, at, :].astype(f32)
        out[...] = y.astype(out.dtype)


def apply_forward(src, blocks, order, add):
    xs = [split(src[:, cols_at(order(i))]) for i in range(NB)]
    ys = []
    for i in range(NB):
        y = lax.dot_general(xs[i], blocks(i), (((1,), (1,)), ((), ())), preferred_element_type=f32)
        h = y.shape[0] // 2
        ys.append(y[:h] + y[h:] + add(i))
    return ys


def apply_adjoint(xs, blocks):
    ys = []
    for i in range(NB):
        y = lax.dot_general(split(xs[i]), blocks(i), (((1,), (0,)), ((), ())), preferred_element_type=f32)
        h = y.shape[0] // 2
        ys.append(y[:h] + y[h:])
    return ys


def cut(x, i):
    return x[:, i * BLK : (i + 1) * BLK]


def block_of(both, t):
    return lambda i: both[t, i * BLK : (i + 1) * BLK]


def assemble(force, own, oth):
    co = lax.axis_index("co")
    half = COLS // 2
    for src, place in ((own, co), (oth, 1 - co)):
        at = pl.ds(pl.multiple_of(place * half, half), half)
        for t in range(2):
            force[t, :, at] = src[:, t * half : (t + 1) * half].astype(f32)
    return force[0], force[1]


def total_kernel(own, oth, both, ords, out, force, tot, tmp):
    z = lax.axis_index("z")
    first, second = assemble(force, own, oth)
    low = force.at[0]
    ys = apply_adjoint([cut(second, i) for i in range(NB)], block_of(both, 1))
    fs = apply_forward(low, block_of(both, 1), lambda i: ords[1, i], lambda i: cut(second, i))
    for i in range(NB):
        tmp[:, cols_at(ords[1, i])] = ys[i]
    back = tmp[...] + first
    ys = apply_adjoint([cut(back, i) for i in range(NB)], block_of(both, 0))
    for i in range(NB):
        tot[:, cols_at(ords[0, i])] = ys[i].astype(bf16)
    adj = tot[...]
    fwd = jnp.concatenate(fs, axis=1).astype(bf16)
    for d in range(out.shape[0]):
        out[d] = jnp.where(d > z, fwd, adj)


def sweep_kernel(recv, stored, tags, both, ords, own, oth, keep, send, maps, st, adj, res, split_force, sem):
    co = lax.axis_index("co")
    z = lax.axis_index("z")
    nz = recv.shape[0]

    def copy(k):
        return pltpu.make_async_copy(stored.at[k], maps.at[k], sem.at[k])

    for j in range(1, nz // 2):
        for k in (j, nz - 1 - j):

            @pl.when(k != z)
            def _():
                copy(k).start()

    force = assemble(split_force, own, oth)
    st[...] = jnp.where(z > 0, recv[0].astype(f32), 0.0)
    adj[...] = jnp.where(z < nz - 1, recv[nz - 1].astype(f32), 0.0)

    def block(k):
        return lambda i: maps[k, i * BLK : (i + 1) * BLK]

    def forward(k, carry):
        copy(k).wait()
        ys = apply_forward(
            st, block(k), lambda i: tags[k, i], lambda i: recv[k, :, i * BLK : (i + 1) * BLK].astype(f32)
        )
        for i in range(NB):
            st[:, i * BLK : (i + 1) * BLK] = ys[i]
        return carry

    def backward(s, carry):
        k = nz - 1 - s
        copy(k).wait()
        ys = apply_adjoint([adj[:, i * BLK : (i + 1) * BLK] for i in range(NB)], block(k))
        more = [recv[k, :, cols_at(tags[k, i])].astype(f32) for i in range(NB)]
        for i in range(NB):
            adj[:, cols_at(tags[k, i])] = ys[i] + more[i]
        return carry

    lax.fori_loop(1, z, forward, 0)
    lax.fori_loop(1, nz - 1 - z, backward, 0)
    up = adj[...] + force[1]
    x0 = apply_forward(st, block_of(both, 0), lambda i: ords[0, i], lambda i: cut(force[0], i))
    y1 = apply_adjoint([cut(up, i) for i in range(NB)], block_of(both, 1))
    for i in range(NB):
        res[0, 0, :, i * BLK : (i + 1) * BLK] = x0[i]
    for i in range(NB):
        res[1, 1, :, cols_at(ords[1, i])] = y1[i]
    up = res[1, 1] + force[0]
    x1 = apply_forward(res.at[0, 0], block_of(both, 1), lambda i: ords[1, i], lambda i: cut(force[1], i))
    y0 = apply_adjoint([cut(up, i) for i in range(NB)], block_of(both, 0))
    for i in range(NB):
        res[1, 0, :, i * BLK : (i + 1) * BLK] = x1[i]
    for i in range(NB):
        res[0, 1, :, cols_at(ords[0, i])] = y0[i]
    keep[...] = res[co]
    send[...] = res[1 - co].astype(bf16)


def join_kernel(keep, back, x, y):
    co = lax.axis_index("co")
    h = keep.shape[1]
    for j, out in enumerate((x, y)):
        out[0, pl.ds(pl.multiple_of(co * h, h), h), :] = keep[j]
        out[0, pl.ds(pl.multiple_of((1 - co) * h, h), h), :] = back[j].astype(f32)


def on_device(anomalies, localization, innovations, obs_cell, tangent_blocks, tangent_order):
    cells, half_cols = anomalies.shape
    n_lon = lax.axis_size("lon")
    nz = lax.axis_size("z")
    shape = jax.ShapeDtypeStruct
    swap = [(0, 1), (1, 0)]
    scale = float(cells * n_lon) ** (-0.5)

    head, tail, own_map = call(
        entry_kernel,
        [
            shape((BLK, half_cols), bf16),
            shape((BLK, half_cols), bf16),
            shape((MSG, BLK), bf16),
        ],
        [HBM] * 5,
        [
            pltpu.VMEM(innovations.shape, f32),
            pltpu.VMEM(obs_cell.shape, jnp.int32),
            pltpu.VMEM((2, BLK, half_cols), bf16),
            pltpu.VMEM((COLS, BLK), f32),
            pltpu.SMEM(tangent_order.shape, jnp.int32),
            pltpu.SemaphoreType.DMA((6,)),
        ],
        flops=10**6,
        data=2 * 10**6,
    )(innovations, obs_cell, anomalies, tangent_blocks.reshape(COLS, BLK), tangent_order)
    up = [(i, (i + 1) % n_lon) for i in range(n_lon)]
    down = [(b, a) for a, b in up]
    fetched = lax.ppermute(anomalies, ("co", "ens"), [(0, 1), (3, 2)])
    before = lax.ppermute(tail, "lon", up)
    after = lax.ppermute(head, "lon", down)
    oth_map = lax.ppermute(own_map, "co", swap)

    both, comp, ords = call(
        map_kernel,
        [shape((2, COLS, BLK), bf16), shape((MSG, BLK), bf16), shape((8, BLK), jnp.int32)],
        [VM, VM],
        [pltpu.VMEM((8, BLK), jnp.int32), pltpu.SemaphoreType.DMA],
        flops=10**7,
        data=2 * 10**6,
        specs=[VM, VM, SM],
    )(own_map, oth_map)
    around = []
    for k in range(nz):
        around.append((k * 2, (k + 1) % nz * 2))
        around.append(((k + 1) % nz * 2 + 1, k * 2 + 1))
    got = []
    held = comp
    for _ in range(1, nz // 2 + 1):
        held = lax.ppermute(held, ("z", "co"), around)
        got.append(held)

    weighted, anom_v, loc_v = call(
        inner_kernel,
        [shape((cells, half_cols), bf16), shape(anomalies.shape, bf16), shape(localization.shape, bf16)],
        [HBM] * 4,
        [pltpu.VMEM(innovations.shape, f32), pltpu.VMEM(obs_cell.shape, jnp.int32), pltpu.SemaphoreType.DMA((4,))],
        flops=10**6,
        data=4 * 10**6,
    )(innovations, obs_cell, anomalies, localization)
    (local,) = call(local_kernel, [shape((cells, half_cols), bf16)], [VM] * 4, flops=10**9, data=4 * 10**6)(
        before, weighted, after, loc_v
    )
    local_oth = lax.ppermute(local, "co", swap)
    (p_all,) = call(
        functools.partial(product_kernel, scale), [shape((half_cols, COLS), bf16)], [VM] * 4, flops=10**9, data=3 * 10**6
    )(local, local_oth, anom_v, fetched)
    rows = half_cols // n_lon
    parts = lax.all_to_all(p_all, "lon", 0, 0, tiled=True).reshape(n_lon, rows, COLS)

    hr = rows // 2
    f_own, f_send = call(
        sum_kernel, [shape((hr, COLS), f32), shape((hr, COLS), bf16)], [VM], flops=10**6, data=10**6
    )(parts)
    f_oth = lax.ppermute(f_send, "co", swap)
    (msgs,) = call(
        total_kernel,
        [shape((nz, hr, COLS), bf16)],
        [VM, VM, VM, SM],
        [pltpu.VMEM((2, hr, COLS), f32), pltpu.VMEM((hr, COLS), bf16), pltpu.VMEM((hr, COLS), f32)],
        flops=10**8,
        data=10**6,
    )(f_own, f_oth, both, ords)
    recv = lax.all_to_all(msgs, "z", 0, 0, tiled=True)

    tied = lax.optimization_barrier((msgs, *got))
    got = list(tied[1:])
    for j in range(nz // 2 - 1):
        got.append(lax.ppermute(got[j], "co", swap))
    maps, table = call(
        arrange_kernel,
        [shape((nz, COLS, BLK), bf16), shape((nz, BLK), jnp.int32)],
        [VM] * len(got),
        [pltpu.VMEM((nz, BLK), jnp.int32), pltpu.SemaphoreType.DMA],
        flops=10**6,
        data=4 * 10**6,
        specs=[VM, SM],
    )(*got)
    keep, send = call(
        sweep_kernel,
        [shape((2, hr, COLS), f32), shape((2, hr, COLS), bf16)],
        [VM, HBM, SM, VM, SM, VM, VM],
        [
            pltpu.VMEM((nz, COLS, BLK), bf16),
            pltpu.VMEM((hr, COLS), f32),
            pltpu.VMEM((hr, COLS), f32),
            pltpu.VMEM((2, 2, hr, COLS), f32),
            pltpu.VMEM((2, hr, COLS), f32),
            pltpu.SemaphoreType.DMA((nz,)),
        ],
        flops=10**9,
        data=3 * 10**6,
    )(recv, maps, table, both, ords, f_own, f_oth)
    back = lax.ppermute(send, "co", swap)
    x, y = call(join_kernel, [shape((1, rows, COLS), f32)] * 2, [VM] * 2, flops=10**6, data=10**6)(keep, back)
    return x, y


def solution(mesh):
    tm, lon, ens = (mesh.shape[a] for a in ("tm", "lon", "ens"))
    fine = Mesh(mesh.devices.reshape(tm // 2, 2, lon, ens), ("z", "co", "lon", "ens"))
    time = ("z", "co")
    placed = (
        P("lon", "ens"),
        P("lon", None, None, None),
        P(time, "lon"),
        P(time, "lon"),
        P(time, None, None, None),
        P(time, None),
    )
    outs = P(time, ("ens", "lon"), None)

    return jax.shard_map(on_device, mesh=fine, in_specs=placed, out_specs=(outs, outs), check_vma=False)
```

```python
import functools

import jax
import jax.numpy as jnp
from jax import lax
from jax.experimental import pallas as pl
from jax.experimental.pallas import tpu as pltpu
from jax.sharding import Mesh
from jax.sharding import PartitionSpec as P

BLK = 128
NB = 8
COLS = NB * BLK
bf16 = jnp.bfloat16
f32 = jnp.float32
i32 = jnp.int32

VM = pl.BlockSpec(memory_space=pltpu.VMEM)
SM = pl.BlockSpec(memory_space=pltpu.SMEM)
HBM = pl.BlockSpec(memory_space=pltpu.HBM)
MIB = 1024 * 1024
NT = (((1,), (1,)), ((), ()))


def call(kernel, outs, ins, scratch=(), flops=0, data=0, grant=16, specs=None):
    made = pl.pallas_call(
        kernel,
        out_shape=outs,
        in_specs=ins,
        out_specs=specs or [VM] * len(outs),
        scratch_shapes=list(scratch),
        compiler_params=pltpu.CompilerParams(vmem_limit_bytes=grant * MIB),
        cost_estimate=pl.CostEstimate(flops=flops, bytes_accessed=data, transcendentals=0),
    )

    def run(*args):
        args = [pltpu.with_memory_space_constraint(a, pltpu.HBM) if i is HBM else a for a, i in zip(args, ins)]
        return made(*args)

    return run


def cols_at(i):
    return pl.ds(pl.multiple_of(i * BLK, BLK), BLK)


def rows_at(i, n):
    return pl.ds(pl.multiple_of(i * n, n), n)


def copies_of(pairs, sem):
    out = [pltpu.make_async_copy(a, b, sem.at[i]) for i, (a, b) in enumerate(pairs)]
    for c in out:
        c.start()
    return out


def entry_kernel(innov, cell, order, anom, loc, spread, up, down, piece, innov_v, cell_v, order_s, edge, ends, sem):
    co = lax.axis_index("co")
    cells = anom.shape[0]
    n = loc.shape[0]
    h = piece.shape[0]
    copies = copies_of(
        (
            (innov, innov_v),
            (cell, cell_v),
            (order, order_s),
            (anom.at[pl.ds(cells - BLK, BLK)], edge.at[0]),
            (anom.at[pl.ds(0, BLK)], edge.at[1]),
            (loc.at[n - 1, 2], ends.at[0]),
            (loc.at[0, 0], ends.at[1]),
            (anom.at[rows_at(co, h)], piece),
        ),
        sem,
    )
    for c in copies[:3]:
        c.wait()
    x = innov_v[...]
    hi = x.astype(bf16)
    mid = (x - hi.astype(f32)).astype(bf16)
    lo = (x - hi.astype(f32) - mid.astype(f32)).astype(bf16)
    rows = jnp.concatenate([hi, mid, lo, jnp.zeros((5, x.shape[1]), bf16)], axis=0)
    ids = lax.broadcasted_iota(i32, (cells, 1), 0)
    hit = jnp.where(ids == cell_v[...], 1.0, 0.0).astype(bf16)
    y = lax.dot_general(rows, hit, NT, preferred_element_type=f32)
    w = y[0:1] + y[1:2] + y[2:3]
    lane = lax.broadcasted_iota(i32, (8, BLK), 1)
    tag = jnp.zeros((8, BLK), f32)
    for i in range(NB):
        tag = jnp.where(lane == i, order_s[0, i].astype(f32), tag)
    one = jnp.concatenate([w[:, i * BLK : (i + 1) * BLK] for i in range(cells // BLK)] + [tag], axis=0)
    for k in range(spread.shape[0]):
        spread[k] = one
    for c in copies[3:]:
        c.wait()
    half = edge.shape[2]
    for j, out in enumerate((up, down)):
        out[:, :half] = edge[j]
        out[:, half:] = ends[j]


def plan_kernel(recv, tang, wt, blocks, traj, tang_v, ints, order_s, traj_s, sem):
    z = lax.axis_index("z")
    co = lax.axis_index("co")
    steps = recv.shape[0]
    (c,) = copies_of(((tang, tang_v),), sem)
    for k in range(steps):
        ints[k : k + 1] = recv[k, 8:9, :].astype(i32)
    d = pltpu.make_async_copy(ints, order_s, sem.at[1])
    d.start()
    pad = jnp.zeros((BLK - steps, BLK), f32)
    for i in range(8):
        part = jnp.concatenate([recv[:, i, :], pad], axis=0)
        wt[i * BLK : (i + 1) * BLK] = part.T
    d.wait()
    for q in range(NB):
        b = jnp.int32(q)
        for t in range(steps - 1, -1, -1):
            traj[t + 1, q] = b
            b = order_s[t, b]
        traj[0, q] = b
    mine = 2 * z + co + 1
    c.wait()
    for q in range(NB):
        blocks[q] = tang_v[traj[mine, q]].astype(bf16)


def ready_kernel(anom, loc, up0, up1, down0, down1, lt, gown, asel, anom_v, loc_v, pad, sem):
    co = lax.axis_index("co")
    copies = copies_of(((loc, loc_v), (anom, anom_v)), sem)
    n = loc.shape[0]
    half = anom.shape[1]
    before = jnp.where(co == 0, up0[:, :half], up1[:, :half])
    after = jnp.where(co == 0, down0[:, :half], down1[:, :half])
    copies[0].wait()
    for b in range(n):
        prev = up0[:, half:] if b == 0 else loc_v[b - 1, 2]
        nxt = down0[:, half:] if b == n - 1 else loc_v[b + 1, 0]
        lt[b] = jnp.concatenate([prev.T, loc_v[b, 1].T, nxt.T], axis=1)
    copies[1].wait()
    pad[:BLK] = before
    pad[BLK : BLK + n * BLK] = anom_v[...]
    pad[BLK + n * BLK :] = after
    for b in range(n):
        y = jnp.dot(lt[b], pad[b * BLK : (b + 3) * BLK], preferred_element_type=f32)
        gown[b * BLK : (b + 1) * BLK] = y.astype(bf16)
    at = anom_v[...].T
    for k in range(half // 64):
        asel[k * 32 : (k + 1) * 32] = jnp.where(co == 0, at[k * 64 : k * 64 + 32], at[k * 64 + 32 : (k + 1) * 64])


def product_kernel(scale, near, far, up0, up1, down0, down1, lt, gown, asel, wt, traj, out, pad, full, vals):
    co = lax.axis_index("co")
    e = lax.axis_index("ens")
    z = lax.axis_index("z")
    h, half = near.shape
    n = lt.shape[0]
    pad[:BLK] = jnp.where(co == 0, up1[:, :half], up0[:, :half])
    pad[pl.ds(pl.multiple_of(BLK + co * h, BLK), h)] = near[...]
    pad[pl.ds(pl.multiple_of(BLK + (1 - co) * h, BLK), h)] = far[...]
    pad[BLK + n * BLK :] = jnp.where(co == 0, down1[:, :half], down0[:, :half])
    there = pl.ds(pl.multiple_of((1 - e) * half, half), half)
    full[:, pl.ds(pl.multiple_of(e * half, half), half)] = gown[...]
    for b in range(n):
        y = jnp.dot(lt[b], pad[b * BLK : (b + 3) * BLK], preferred_element_type=f32)
        full[b * BLK : (b + 1) * BLK, there] = y.astype(bf16)
    steps = vals.shape[1] // BLK
    group = 4
    for g in range(0, steps, group):
        for t in range(g, g + group):
            y = wt[:, t : t + 1] * full[:, cols_at(traj[t + 1, z])].astype(f32)
            vals[:, t * BLK : (t + 1) * BLK] = y.astype(bf16)
        at = slice(g * BLK, (g + group) * BLK)
        y = jnp.dot(asel[...], vals[:, at], preferred_element_type=f32)
        out[:, at] = (y * scale).astype(bf16)


def split(x):
    hi = x.astype(bf16)
    lo = (x - hi.astype(f32)).astype(bf16)
    return jnp.concatenate([hi, lo], axis=0)


def times(x, block, transposed):
    dims = NT if transposed else (((1,), (0,)), ((), ()))
    y = lax.dot_general(split(x), block, dims, preferred_element_type=f32)
    rows = x.shape[0]
    return y[:rows] + y[rows:]


def scan_kernel(parts, mine, theirs, out):
    co = lax.axis_index("co")
    n = parts.shape[0]
    steps = parts.shape[2] // BLK
    even = jnp.where(co == 0, mine[...], theirs[...])
    odd = jnp.where(co == 0, theirs[...], mine[...])
    blocks = [(even if t % 2 == 0 else odd)[t // 2] for t in range(steps)]
    force = []
    for t in range(steps):
        at = slice(t * BLK, (t + 1) * BLK)
        y = parts[0, :, at].astype(f32)
        for s in range(1, n):
            y = y + parts[s, :, at].astype(f32)
        force.append(y)
    x = force[0]
    y = times(force[steps - 1], blocks[steps - 1], False)
    out[0, 0] = x.astype(bf16)
    out[steps - 1, 1] = y.astype(bf16)
    for k in range(1, steps):
        t = steps - 1 - k
        x = times(x, blocks[k], True) + force[k]
        y = times(y + force[t], blocks[t], False)
        out[k, 0] = x.astype(bf16)
        out[t, 1] = y.astype(bf16)


def place_kernel(recv, traj, x, y):
    t = 2 * lax.axis_index("z") + lax.axis_index("co")
    rows = recv.shape[2]
    for q in range(NB):
        for c in range(2):
            at = slice(c * rows, (c + 1) * rows)
            x[0, at, cols_at(traj[t + 1, q])] = recv[2 * q + c, 0].astype(f32)
            y[0, at, cols_at(traj[t, q])] = recv[2 * q + c, 1].astype(f32)


def on_device(anomalies, localization, innovations, obs_cell, tangent_blocks, tangent_order):
    cells, half = anomalies.shape
    n_lon = lax.axis_size("lon")
    nz = lax.axis_size("z")
    steps = 2 * nz
    shape = jax.ShapeDtypeStruct
    swap = [(0, 1), (1, 0)]
    scale = float(cells * n_lon) ** (-0.5)
    n = cells // BLK
    time = ("z", "co")

    spread, tail, head, piece = call(
        entry_kernel,
        [
            shape((steps, 16, BLK), f32),
            shape((BLK, half + BLK), bf16),
            shape((BLK, half + BLK), bf16),
            shape((cells // 2, half), bf16),
        ],
        [HBM] * 5,
        [
            pltpu.VMEM(innovations.shape, f32),
            pltpu.VMEM(obs_cell.shape, i32),
            pltpu.SMEM(tangent_order.shape, i32),
            pltpu.VMEM((2, BLK, half), bf16),
            pltpu.VMEM((2, BLK, BLK), bf16),
            pltpu.SemaphoreType.DMA((8,)),
        ],
        flops=10**7,
        data=10**6,
    )(innovations, obs_cell, tangent_order, anomalies, localization)

    upward, downward = [], []
    for c in range(2):
        for k in range(n_lon):
            for e in range(2):
                f = e if c == 0 else 1 - e
                k2 = (k + 1) % n_lon
                upward.append(((c * n_lon + k) * 2 + e, (c * n_lon + k2) * 2 + f))
                downward.append(((c * n_lon + k2) * 2 + e, (c * n_lon + k) * 2 + f))
    up0 = lax.ppermute(tail, ("co", "lon", "ens"), upward)
    down0 = lax.ppermute(head, ("co", "lon", "ens"), downward)
    near = lax.ppermute(piece, "ens", swap)
    recv = lax.all_to_all(spread, time, 0, 0, tiled=True)
    wt, blocks, traj = call(
        plan_kernel,
        [shape((cells, BLK), f32), shape((NB, BLK, BLK), bf16), shape((steps + 1, NB), i32)],
        [VM, HBM],
        [
            pltpu.VMEM((NB, BLK, BLK), f32),
            pltpu.VMEM((steps, BLK), i32),
            pltpu.SMEM((steps, BLK), i32),
            pltpu.SMEM((8, BLK), i32),
            pltpu.SemaphoreType.DMA((2,)),
        ],
        flops=10**6,
        data=10**6,
        specs=[VM, VM, SM],
    )(recv, tangent_blocks.reshape(NB, BLK, BLK))
    mine = lax.all_to_all(blocks, "z", 0, 0, tiled=True)

    up1 = lax.ppermute(up0, "co", swap)
    down1 = lax.ppermute(down0, "co", swap)
    lt, gown, asel = call(
        ready_kernel,
        [shape((n, BLK, 3 * BLK), bf16), shape((cells, half), bf16), shape((half // 2, cells), bf16)],
        [HBM, HBM, VM, VM, VM, VM],
        [
            pltpu.VMEM(anomalies.shape, bf16),
            pltpu.VMEM(localization.shape, bf16),
            pltpu.VMEM((cells + 2 * BLK, half), bf16),
            pltpu.SemaphoreType.DMA((2,)),
        ],
        flops=10**9,
        data=4 * 10**6,
    )(anomalies, localization, up0, up1, down0, down1)
    far = lax.ppermute(near, "co", swap)
    (prod,) = call(
        functools.partial(product_kernel, scale),
        [shape((half // 2, steps * BLK), bf16)],
        [VM] * 10 + [SM],
        [
            pltpu.VMEM((cells + 2 * BLK, half), bf16),
            pltpu.VMEM((cells, COLS), bf16),
            pltpu.VMEM((cells, steps * BLK), bf16),
        ],
        flops=10**9,
        data=4 * 10**6,
        grant=24,
    )(near, far, up0, up1, down0, down1, lt, gown, asel, wt, traj)
    rows = half // 2 // n_lon
    parts = lax.all_to_all(prod, "lon", 0, 0, tiled=True).reshape(n_lon, rows, steps * BLK)
    theirs = lax.ppermute(mine, "co", swap)
    (states,) = call(
        scan_kernel, [shape((steps, 2, rows, BLK), bf16)], [VM] * 3, flops=10**9, data=2 * 10**6
    )(parts, mine, theirs)
    back = lax.all_to_all(states, time, 0, 0, tiled=True)
    x, y = call(place_kernel, [shape((1, 2 * rows, COLS), f32)] * 2, [VM, SM], flops=10**6, data=10**6)(back, traj)
    return x, y


def solution(mesh):
    tm, lon, ens = (mesh.shape[a] for a in ("tm", "lon", "ens"))
    fine = Mesh(mesh.devices.reshape(tm // 2, 2, lon, ens), ("z", "co", "lon", "ens"))
    time = ("z", "co")
    placed = (
        P("lon", "ens"),
        P("lon", None, None, None),
        P(time, "lon"),
        P(time, "lon"),
        P(time, None, None, None),
        P(time, None),
    )
    outs = P(time, ("ens", "lon"), None)

    return jax.shard_map(on_device, mesh=fine, in_specs=placed, out_specs=(outs, outs), check_vma=False)
```

```python
import functools

import jax
import jax.numpy as jnp
from jax import lax
from jax.experimental import pallas as pl
from jax.experimental.pallas import tpu as pltpu
from jax.sharding import Mesh
from jax.sharding import PartitionSpec as P

BLK = 128
NB = 8
COLS = NB * BLK
bf16 = jnp.bfloat16
f32 = jnp.float32
i32 = jnp.int32

VM = pl.BlockSpec(memory_space=pltpu.VMEM)
SM = pl.BlockSpec(memory_space=pltpu.SMEM)
HBM = pl.BlockSpec(memory_space=pltpu.HBM)
MIB = 1024 * 1024
WT = f32
NT = (((1,), (1,)), ((), ()))


def call(kernel, outs, ins, scratch=(), flops=0, data=0, grant=16, specs=None):
    made = pl.pallas_call(
        kernel,
        out_shape=outs,
        in_specs=ins,
        out_specs=specs or [VM] * len(outs),
        scratch_shapes=list(scratch),
        compiler_params=pltpu.CompilerParams(vmem_limit_bytes=grant * MIB),
        cost_estimate=pl.CostEstimate(flops=flops, bytes_accessed=data, transcendentals=0),
    )

    def run(*args):
        args = [pltpu.with_memory_space_constraint(a, pltpu.HBM) if i is HBM else a for a, i in zip(args, ins)]
        return made(*args)

    return run


def cols_at(i):
    return pl.ds(pl.multiple_of(i * BLK, BLK), BLK)


def rows_at(i, n):
    return pl.ds(pl.multiple_of(i * n, n), n)


def copies_of(pairs, sem):
    out = [pltpu.make_async_copy(a, b, sem.at[i]) for i, (a, b) in enumerate(pairs)]
    for c in out:
        c.start()
    return out


def entry_kernel(
    innov, cell, order, anom, loc, tang, spread, up, down, piece, own, innov_v, cell_v, order_s, edge, ends, tang_v, sem
):
    co = lax.axis_index("co")
    cells = anom.shape[0]
    n = loc.shape[0]
    h = piece.shape[0]
    copies = copies_of(
        (
            (innov, innov_v),
            (cell, cell_v),
            (order, order_s),
            (anom.at[pl.ds(cells - BLK, BLK)], edge.at[0]),
            (anom.at[pl.ds(0, BLK)], edge.at[1]),
            (loc.at[n - 1, 2], ends.at[0]),
            (loc.at[0, 0], ends.at[1]),
            (anom.at[rows_at(co, h)], piece),
            (tang, tang_v),
        ),
        sem,
    )
    for c in copies[:3]:
        c.wait()
    x = innov_v[...]
    hi = x.astype(bf16)
    mid = (x - hi.astype(f32)).astype(bf16)
    lo = (x - hi.astype(f32) - mid.astype(f32)).astype(bf16)
    rows = jnp.concatenate([hi, mid, lo, jnp.zeros((5, x.shape[1]), bf16)], axis=0)
    ids = lax.broadcasted_iota(i32, (cells, 1), 0)
    hit = jnp.where(ids == cell_v[...], 1.0, 0.0).astype(bf16)
    y = lax.dot_general(rows, hit, NT, preferred_element_type=f32)
    w = y[0:1] + y[1:2] + y[2:3]
    lane = lax.broadcasted_iota(i32, (8, BLK), 1)
    tag = jnp.zeros((8, BLK), f32)
    for i in range(NB):
        tag = jnp.where(lane == i, order_s[0, i].astype(f32), tag)
    one = jnp.concatenate([w[:, i * BLK : (i + 1) * BLK] for i in range(cells // BLK)] + [tag], axis=0)
    for k in range(spread.shape[0]):
        spread[k] = one
    for c in copies[3:]:
        c.wait()
    half = edge.shape[2]
    for j, out in enumerate((up, down)):
        out[:, :half] = edge[j]
        out[:, half:] = ends[j]
    own[...] = tang_v[...].astype(bf16)


def choose_kernel(own, oth, recv, traj, *refs):
    *outs, ints, order_s, picked, sem = refs
    z = lax.axis_index("z")
    co = lax.axis_index("co")
    steps = recv.shape[0]
    nz = steps // 2
    for k in range(steps):
        ints[k : k + 1] = recv[k, 8:9, :].astype(i32)
    d = pltpu.make_async_copy(ints, order_s, sem.at[0])
    d.start()
    d.wait()
    for q in range(NB):
        b = jnp.int32(q)
        for t in range(steps - 1, -1, -1):
            traj[t + 1, q] = b
            b = order_s[t, b]
        traj[0, q] = b
    copies = []
    for d, out in enumerate(outs):
        q = lax.rem(jnp.where(co == 0, z + d, z + nz - d), nz)
        copies.append((own.at[traj[2 * z + co + 1, q]], picked.at[d]))
        if d < nz // 2:
            copies.append((oth.at[traj[2 * z + 2 - co, q]], out.at[1 - co]))
    for c in copies_of(copies, sem.at[pl.ds(1, len(copies))]):
        c.wait()
    for d, out in enumerate(outs):
        if d < nz // 2:
            out[co] = picked[d].astype(bf16)
        else:
            out[...] = picked[d].astype(bf16)


def ready_kernel(anom, loc, up0, up1, down0, down1, lt, gown, asel, ends, anom_v, loc_v, pad, sem):
    co = lax.axis_index("co")
    copies = copies_of(((loc, loc_v), (anom, anom_v)), sem)
    n = loc.shape[0]
    half = anom.shape[1]
    before = jnp.where(co == 0, up0[:, :half], up1[:, :half])
    after = jnp.where(co == 0, down0[:, :half], down1[:, :half])
    ends[0] = jnp.where(co == 0, up1[:, :half], up0[:, :half])
    ends[1] = jnp.where(co == 0, down1[:, :half], down0[:, :half])
    copies[0].wait()
    for b in range(n):
        prev = up0[:, half:] if b == 0 else loc_v[b - 1, 2]
        nxt = down0[:, half:] if b == n - 1 else loc_v[b + 1, 0]
        lt[b] = jnp.concatenate([prev.T, loc_v[b, 1].T, nxt.T], axis=1)
    copies[1].wait()
    pad[:BLK] = before
    pad[BLK : BLK + n * BLK] = anom_v[...]
    pad[BLK + n * BLK :] = after
    for b in range(n):
        y = jnp.dot(lt[b], pad[b * BLK : (b + 3) * BLK], preferred_element_type=f32)
        gown[b * BLK : (b + 1) * BLK] = y.astype(bf16)
    at = anom_v[...].T
    for k in range(half // 64):
        asel[k * 32 : (k + 1) * 32] = jnp.where(co == 0, at[k * 64 : k * 64 + 32], at[k * 64 + 32 : (k + 1) * 64])


def product_kernel(scale, near, far, ends, lt, gown, asel, recv, out, pad, full, vals, wt, ints, order_s, sem):
    co = lax.axis_index("co")
    e = lax.axis_index("ens")
    z = lax.axis_index("z")
    steps = recv.shape[0]
    for k in range(steps):
        ints[k : k + 1] = recv[k, 8:9, :].astype(i32)
    h, half = near.shape
    n = lt.shape[0]
    d, up, down = copies_of(
        (
            (ints, order_s),
            (ends.at[0], pad.at[pl.ds(0, BLK)]),
            (ends.at[1], pad.at[pl.ds(BLK + n * BLK, BLK)]),
        ),
        sem,
    )
    pad[pl.ds(pl.multiple_of(BLK + co * h, BLK), h)] = near[...]
    pad[pl.ds(pl.multiple_of(BLK + (1 - co) * h, BLK), h)] = far[...]
    there = pl.ds(pl.multiple_of((1 - e) * half, half), half)
    full[:, pl.ds(pl.multiple_of(e * half, half), half)] = gown[...]
    blank = jnp.zeros((BLK - steps, BLK), f32)
    up.wait()
    down.wait()
    for b in range(n):
        y = jnp.dot(lt[b], pad[b * BLK : (b + 3) * BLK], preferred_element_type=f32)
        full[b * BLK : (b + 1) * BLK, there] = y.astype(bf16)
        wt[b * BLK : (b + 1) * BLK] = jnp.concatenate([recv[:, b, :], blank], axis=0).T.astype(wt.dtype)
    d.wait()
    at = [None] * steps
    b = z
    for t in range(steps - 1, -1, -1):
        at[t] = cols_at(b)
        b = order_s[t, b]
    group = 4
    for g in range(0, steps, group):
        for t in range(g, g + group):
            y = wt[:, t : t + 1] * full[:, at[t]].astype(wt.dtype)
            vals[:, t * BLK : (t + 1) * BLK] = y.astype(bf16)
        cols = slice(g * BLK, (g + group) * BLK)
        y = jnp.dot(asel[...], vals[:, cols], preferred_element_type=f32)
        out[:, cols] = (y * scale).astype(bf16)


def split(x):
    hi = x.astype(bf16)
    lo = (x - hi.astype(f32)).astype(bf16)
    return jnp.concatenate([hi, lo], axis=0)


def times(x, block, transposed):
    dims = NT if transposed else (((1,), (0,)), ((), ()))
    y = lax.dot_general(split(x), block, dims, preferred_element_type=f32)
    rows = x.shape[0]
    return y[:rows] + y[rows:]


def scan_kernel(parts, *refs):
    *held, out, blocks = refs
    co = lax.axis_index("co")
    z = lax.axis_index("z")
    n = parts.shape[0]
    steps = parts.shape[2] // BLK
    nz = steps // 2
    h = nz // 2
    for d in range(h):
        for j, src in enumerate((held[d], held[h + d]) if d else (held[0],)):
            back = (co == 0) if j == 0 else (co == 1)
            k = lax.rem(jnp.where(back, z + nz - d, z + d), nz)
            blocks[pl.ds(2 * k, 2)] = src[...]
    k = lax.rem(z + h, nz)
    blocks[2 * k + co] = held[2 * h][...]
    blocks[2 * k + 1 - co] = held[2 * h + 1][...]
    force = []
    for t in range(steps):
        at = slice(t * BLK, (t + 1) * BLK)
        y = parts[0, :, at].astype(f32)
        for s in range(1, n):
            y = y + parts[s, :, at].astype(f32)
        force.append(y)
    x = force[0]
    y = times(force[steps - 1], blocks[steps - 1], False)
    out[0, 0] = x.astype(bf16)
    out[steps - 1, 1] = y.astype(bf16)
    for k in range(1, steps):
        t = steps - 1 - k
        x = times(x, blocks[k], True) + force[k]
        y = times(y + force[t], blocks[t], False)
        out[k, 0] = x.astype(bf16)
        out[t, 1] = y.astype(bf16)


def place_kernel(recv, traj, x, y):
    t = 2 * lax.axis_index("z") + lax.axis_index("co")
    rows = recv.shape[2]
    for q in range(NB):
        for c in range(2):
            at = slice(c * rows, (c + 1) * rows)
            x[0, at, cols_at(traj[t + 1, q])] = recv[2 * q + c, 0].astype(f32)
            y[0, at, cols_at(traj[t, q])] = recv[2 * q + c, 1].astype(f32)


def on_device(anomalies, localization, innovations, obs_cell, tangent_blocks, tangent_order):
    cells, half = anomalies.shape
    n_lon = lax.axis_size("lon")
    nz = lax.axis_size("z")
    steps = 2 * nz
    shape = jax.ShapeDtypeStruct
    swap = [(0, 1), (1, 0)]
    scale = float(cells * n_lon) ** (-0.5)
    n = cells // BLK
    time = ("z", "co")

    spread, tail, head, piece, own_blocks = call(
        entry_kernel,
        [
            shape((steps, 16, BLK), f32),
            shape((BLK, half + BLK), bf16),
            shape((BLK, half + BLK), bf16),
            shape((cells // 2, half), bf16),
            shape((NB, BLK, BLK), bf16),
        ],
        [HBM] * 6,
        [
            pltpu.VMEM(innovations.shape, f32),
            pltpu.VMEM(obs_cell.shape, i32),
            pltpu.SMEM(tangent_order.shape, i32),
            pltpu.VMEM((2, BLK, half), bf16),
            pltpu.VMEM((2, BLK, BLK), bf16),
            pltpu.VMEM((NB, BLK, BLK), f32),
            pltpu.SemaphoreType.DMA((9,)),
        ],
        flops=10**7,
        data=10**6,
    )(innovations, obs_cell, tangent_order, anomalies, localization, tangent_blocks.reshape(NB, BLK, BLK))

    upward, downward = [], []
    for c in range(2):
        for k in range(n_lon):
            for e in range(2):
                f = e if c == 0 else 1 - e
                k2 = (k + 1) % n_lon
                upward.append(((c * n_lon + k) * 2 + e, (c * n_lon + k2) * 2 + f))
                downward.append(((c * n_lon + k2) * 2 + e, (c * n_lon + k) * 2 + f))
    up0 = lax.ppermute(tail, ("co", "lon", "ens"), upward)
    down0 = lax.ppermute(head, ("co", "lon", "ens"), downward)
    near = lax.ppermute(piece, "ens", swap)
    recv = lax.all_to_all(spread, time, 0, 0, tiled=True)
    oth_blocks = lax.ppermute(own_blocks, "co", swap)
    count = nz + 1
    traj, *sends = call(
        choose_kernel,
        [shape((steps + 1, NB), i32)] + [shape((2, BLK, BLK), bf16)] * (nz // 2) + [shape((BLK, BLK), bf16)],
        [HBM, HBM, VM],
        [
            pltpu.VMEM((steps, BLK), i32),
            pltpu.SMEM((steps, BLK), i32),
            pltpu.VMEM((nz // 2 + 1, BLK, BLK), f32),
            pltpu.SemaphoreType.DMA((count + 1,)),
        ],
        flops=10**6,
        data=10**6,
        specs=[SM] + [VM] * (nz // 2 + 1),
    )(tangent_blocks.reshape(NB, BLK, BLK), oth_blocks, recv)
    got = []
    for d in range(1, nz // 2):
        pairs = []
        for k in range(nz):
            pairs.append((2 * k, (k + d) % nz * 2))
            pairs.append((2 * k + 1, (k - d) % nz * 2 + 1))
        got.append(lax.ppermute(sends[d], time, pairs))
    last = lax.ppermute(sends[nz // 2], "z", [(k, (k + nz // 2) % nz) for k in range(nz)])
    crossed = []
    for g in got + [last]:
        crossed.append(lax.ppermute(g, "co", swap))
    held = [sends[0], *got, sends[0], *crossed[:-1], last, crossed[-1]]

    up1 = lax.ppermute(up0, "co", swap)
    down1 = lax.ppermute(down0, "co", swap)
    lt, gown, asel, ends = call(
        ready_kernel,
        [
            shape((n, BLK, 3 * BLK), bf16),
            shape((cells, half), bf16),
            shape((half // 2, cells), bf16),
            shape((2, BLK, half), bf16),
        ],
        [HBM, HBM, VM, VM, VM, VM],
        [
            pltpu.VMEM(anomalies.shape, bf16),
            pltpu.VMEM(localization.shape, bf16),
            pltpu.VMEM((cells + 2 * BLK, half), bf16),
            pltpu.SemaphoreType.DMA((2,)),
        ],
        flops=10**9,
        data=4 * 10**6,
    )(anomalies, localization, up0, up1, down0, down1)
    far = lax.ppermute(near, "co", swap)
    (prod,) = call(
        functools.partial(product_kernel, scale),
        [shape((half // 2, steps * BLK), bf16)],
        [VM, VM, HBM, VM, VM, VM, VM],
        [
            pltpu.VMEM((cells + 2 * BLK, half), bf16),
            pltpu.VMEM((cells, COLS), bf16),
            pltpu.VMEM((cells, steps * BLK), bf16),
            pltpu.VMEM((cells, BLK), WT),
            pltpu.VMEM((steps, BLK), i32),
            pltpu.SMEM((steps, BLK), i32),
            pltpu.SemaphoreType.DMA((3,)),
        ],
        flops=10**9,
        data=4 * 10**6,
        grant=24,
    )(near, far, ends, lt, gown, asel, recv)
    rows = half // 2 // n_lon
    parts = lax.all_to_all(prod, "lon", 0, 0, tiled=True).reshape(n_lon, rows, steps * BLK)
    (states,) = call(
        scan_kernel,
        [shape((steps, 2, rows, BLK), bf16)],
        [VM] * (1 + len(held)),
        [pltpu.VMEM((steps, BLK, BLK), bf16)],
        flops=10**9,
        data=2 * 10**6,
    )(parts, *held)
    back = lax.all_to_all(states, time, 0, 0, tiled=True)
    x, y = call(place_kernel, [shape((1, 2 * rows, COLS), f32)] * 2, [VM, SM], flops=10**6, data=10**6)(back, traj)
    return x, y


def solution(mesh):
    tm, lon, ens = (mesh.shape[a] for a in ("tm", "lon", "ens"))
    fine = Mesh(mesh.devices.reshape(tm // 2, 2, lon, ens), ("z", "co", "lon", "ens"))
    time = ("z", "co")
    placed = (
        P("lon", "ens"),
        P("lon", None, None, None),
        P(time, "lon"),
        P(time, "lon"),
        P(time, None, None, None),
        P(time, None),
    )
    outs = P(time, ("ens", "lon"), None)

    return jax.shard_map(on_device, mesh=fine, in_specs=placed, out_specs=(outs, outs), check_vma=False)
```

```python
import functools

import jax
import jax.numpy as jnp
from jax import lax
from jax.experimental import pallas as pl
from jax.experimental.pallas import tpu as pltpu
from jax.sharding import Mesh
from jax.sharding import PartitionSpec as P

BLK = 128
NB = 8
COLS = NB * BLK
bf16 = jnp.bfloat16
f32 = jnp.float32
i32 = jnp.int32

VM = pl.BlockSpec(memory_space=pltpu.VMEM)
SM = pl.BlockSpec(memory_space=pltpu.SMEM)
HBM = pl.BlockSpec(memory_space=pltpu.HBM)
MIB = 1024 * 1024
NT = (((1,), (1,)), ((), ()))


def call(kernel, outs, ins, scratch=(), flops=0, data=0, grant=16, specs=None):
    made = pl.pallas_call(
        kernel,
        out_shape=outs,
        in_specs=ins,
        out_specs=specs or [VM] * len(outs),
        scratch_shapes=list(scratch),
        compiler_params=pltpu.CompilerParams(vmem_limit_bytes=grant * MIB),
        cost_estimate=pl.CostEstimate(flops=flops, bytes_accessed=data, transcendentals=0),
    )

    def run(*args):
        args = [pltpu.with_memory_space_constraint(a, pltpu.HBM) if i is HBM else a for a, i in zip(args, ins)]
        return made(*args)

    return run


def cols_at(i):
    return pl.ds(pl.multiple_of(i * BLK, BLK), BLK)


def rows_at(i, n):
    return pl.ds(pl.multiple_of(i * n, n), n)


def copies_of(pairs, sem):
    out = [pltpu.make_async_copy(a, b, sem.at[i]) for i, (a, b) in enumerate(pairs)]
    for c in out:
        c.start()
    return out


def entry_kernel(
    innov, cell, order, anom, loc, tang, spread, up, down, piece, own, innov_v, cell_v, order_s, edge, ends, tang_v, sem
):
    co = lax.axis_index("co")
    cells = anom.shape[0]
    n = loc.shape[0]
    h = piece.shape[0]
    copies = copies_of(
        (
            (innov, innov_v),
            (cell, cell_v),
            (order, order_s),
            (anom.at[pl.ds(cells - BLK, BLK)], edge.at[0]),
            (anom.at[pl.ds(0, BLK)], edge.at[1]),
            (loc.at[n - 1, 2], ends.at[0]),
            (loc.at[0, 0], ends.at[1]),
            (anom.at[rows_at(co, h)], piece),
            (tang, tang_v),
        ),
        sem,
    )
    for c in copies[:3]:
        c.wait()
    x = innov_v[...]
    hi = x.astype(bf16)
    mid = (x - hi.astype(f32)).astype(bf16)
    lo = (x - hi.astype(f32) - mid.astype(f32)).astype(bf16)
    rows = jnp.concatenate([hi, mid, lo, jnp.zeros((5, x.shape[1]), bf16)], axis=0)
    ids = lax.broadcasted_iota(i32, (cells, 1), 0)
    hit = jnp.where(ids == cell_v[...], 1.0, 0.0).astype(bf16)
    y = lax.dot_general(rows, hit, NT, preferred_element_type=f32)
    w = y[0:1] + y[1:2] + y[2:3]
    lane = lax.broadcasted_iota(i32, (8, BLK), 1)
    tag = jnp.zeros((8, BLK), f32)
    for i in range(NB):
        tag = jnp.where(lane == i, order_s[0, i].astype(f32), tag)
    one = jnp.concatenate([w[:, i * BLK : (i + 1) * BLK] for i in range(cells // BLK)] + [tag], axis=0)
    for k in range(spread.shape[0]):
        spread[k] = one
    for c in copies[3:]:
        c.wait()
    half = edge.shape[2]
    for j, out in enumerate((up, down)):
        out[:, :half] = edge[j]
        out[:, half:] = ends[j]
    own[...] = tang_v[...].astype(bf16)


def choose_kernel(own, oth, recv, traj, *refs):
    *outs, ints, order_s, picked, sem = refs
    z = lax.axis_index("z")
    co = lax.axis_index("co")
    steps = recv.shape[0]
    nz = steps // 2
    for k in range(steps):
        ints[k : k + 1] = recv[k, 8:9, :].astype(i32)
    d = pltpu.make_async_copy(ints, order_s, sem.at[0])
    d.start()
    d.wait()
    at = [jnp.int32(q) for q in range(NB)]
    for t in range(steps - 1, -1, -1):
        for q in range(NB):
            traj[t + 1, q] = at[q]
        at = [order_s[t, b] for b in at]
    for q in range(NB):
        traj[0, q] = at[q]
    copies = []
    for d, out in enumerate(outs):
        q = lax.rem(jnp.where(co == 0, z + d, z + nz - d), nz)
        copies.append((own.at[traj[2 * z + co + 1, q]], picked.at[d]))
        if d < nz // 2:
            copies.append((oth.at[traj[2 * z + 2 - co, q]], out.at[1 - co]))
    for c in copies_of(copies, sem.at[pl.ds(1, len(copies))]):
        c.wait()
    for d, out in enumerate(outs):
        if d < nz // 2:
            out[co] = picked[d].astype(bf16)
        else:
            out[...] = picked[d].astype(bf16)


def ready_kernel(anom, loc, *refs):
    *edges, lt, gown, asel, ends, anom_v, loc_v, edge_v, pad, sem = refs
    co = lax.axis_index("co")
    pairs = [(a, edge_v.at[i]) for i, a in enumerate(edges)]
    copies = copies_of(((loc, loc_v), (anom, anom_v), *pairs), sem)
    n = loc.shape[0]
    half = anom.shape[1]
    for c in copies[2:]:
        c.wait()
    up0, up1, down0, down1 = (edge_v.at[i] for i in range(4))
    before = jnp.where(co == 0, up0[:, :half], up1[:, :half])
    after = jnp.where(co == 0, down0[:, :half], down1[:, :half])
    ends[0] = jnp.where(co == 0, up1[:, :half], up0[:, :half])
    ends[1] = jnp.where(co == 0, down1[:, :half], down0[:, :half])
    copies[0].wait()
    for b in range(n):
        prev = up0[:, half:] if b == 0 else loc_v[b - 1, 2]
        nxt = down0[:, half:] if b == n - 1 else loc_v[b + 1, 0]
        lt[b] = jnp.concatenate([prev.T, loc_v[b, 1].T, nxt.T], axis=1)
    copies[1].wait()
    pad[:BLK] = before
    pad[BLK : BLK + n * BLK] = anom_v[...]
    pad[BLK + n * BLK :] = after
    for b in range(n):
        y = jnp.dot(lt[b], pad[b * BLK : (b + 3) * BLK], preferred_element_type=f32)
        gown[b * BLK : (b + 1) * BLK] = y.astype(bf16)
    at = anom_v[...].T
    for k in range(half // 64):
        asel[k * 32 : (k + 1) * 32] = jnp.where(co == 0, at[k * 64 : k * 64 + 32], at[k * 64 + 32 : (k + 1) * 64])


def product_kernel(
    scale, near, far, ends, lt, gown, asel, recv, out, pad, full, vals, wt, res, ints, order_s, sem, out_sem
):
    co = lax.axis_index("co")
    e = lax.axis_index("ens")
    z = lax.axis_index("z")
    steps = recv.shape[0]
    for k in range(steps):
        ints[k : k + 1] = recv[k, 8:9, :].astype(i32)
    h, half = near.shape
    n = lt.shape[0]
    there = pl.ds(pl.multiple_of((1 - e) * half, half), half)
    copies = copies_of(
        (
            (near, pad.at[pl.ds(pl.multiple_of(BLK + co * h, BLK), h)]),
            (far, pad.at[pl.ds(pl.multiple_of(BLK + (1 - co) * h, BLK), h)]),
            (ints, order_s),
            (gown, full.at[:, pl.ds(pl.multiple_of(e * half, half), half)]),
        ),
        sem,
    )
    blank = jnp.zeros((BLK - steps, BLK), f32)
    for b in range(n):
        wt[b * BLK : (b + 1) * BLK] = jnp.concatenate([recv[:, b, :], blank], axis=0).T
    pad[:BLK] = ends[0]
    pad[BLK + n * BLK :] = ends[1]
    copies[0].wait()
    copies[1].wait()
    for b in range(n):
        y = jnp.dot(lt[b], pad[b * BLK : (b + 3) * BLK], preferred_element_type=f32)
        full[b * BLK : (b + 1) * BLK, there] = y.astype(bf16)
    copies[2].wait()
    copies[3].wait()
    at = [None] * steps
    b = z
    for t in range(steps - 1, -1, -1):
        at[t] = cols_at(b)
        b = order_s[t, b]
    group = 4
    sent = []
    for g in range(0, steps, group):
        for t in range(g, g + group):
            y = wt[:, t : t + 1] * full[:, at[t]].astype(f32)
            vals[:, t * BLK : (t + 1) * BLK] = y.astype(bf16)
        cols = slice(g * BLK, (g + group) * BLK)
        y = jnp.dot(asel[...], vals[:, cols], preferred_element_type=f32)
        res[:, cols] = (y * scale).astype(bf16)
        c = pltpu.make_async_copy(res.at[:, cols], out.at[:, cols], out_sem.at[g // group])
        c.start()
        sent.append(c)
    for c in sent:
        c.wait()


def split(x):
    hi = x.astype(bf16)
    lo = (x - hi.astype(f32)).astype(bf16)
    return jnp.concatenate([hi, lo], axis=0)


def times(x, block, transposed):
    dims = NT if transposed else (((1,), (0,)), ((), ()))
    y = lax.dot_general(split(x), block, dims, preferred_element_type=f32)
    rows = x.shape[0]
    return y[:rows] + y[rows:]


def scan_kernel(parts, *refs):
    *held, out, blocks = refs
    co = lax.axis_index("co")
    z = lax.axis_index("z")
    n = parts.shape[0]
    steps = parts.shape[2] // BLK
    nz = steps // 2
    h = nz // 2
    for d in range(h):
        for j, src in enumerate((held[d], held[h + d]) if d else (held[0],)):
            back = (co == 0) if j == 0 else (co == 1)
            k = lax.rem(jnp.where(back, z + nz - d, z + d), nz)
            blocks[pl.ds(2 * k, 2)] = src[...]
    k = lax.rem(z + h, nz)
    blocks[2 * k + co] = held[2 * h][...]
    blocks[2 * k + 1 - co] = held[2 * h + 1][...]
    force = []
    for t in range(steps):
        at = slice(t * BLK, (t + 1) * BLK)
        y = parts[0, :, at].astype(f32)
        for s in range(1, n):
            y = y + parts[s, :, at].astype(f32)
        force.append(y)
    x = force[0]
    y = times(force[steps - 1], blocks[steps - 1], False)
    out[0, 0] = x.astype(bf16)
    out[steps - 1, 1] = y.astype(bf16)
    for k in range(1, steps):
        t = steps - 1 - k
        x = times(x, blocks[k], True) + force[k]
        y = times(y + force[t], blocks[t], False)
        out[k, 0] = x.astype(bf16)
        out[t, 1] = y.astype(bf16)


def place_kernel(recv, traj, x, y):
    t = 2 * lax.axis_index("z") + lax.axis_index("co")
    rows = recv.shape[2]
    for q in range(NB):
        for c in range(2):
            at = slice(c * rows, (c + 1) * rows)
            x[0, at, cols_at(traj[t + 1, q])] = recv[2 * q + c, 0].astype(f32)
            y[0, at, cols_at(traj[t, q])] = recv[2 * q + c, 1].astype(f32)


def on_device(anomalies, localization, innovations, obs_cell, tangent_blocks, tangent_order):
    cells, half = anomalies.shape
    n_lon = lax.axis_size("lon")
    nz = lax.axis_size("z")
    steps = 2 * nz
    shape = jax.ShapeDtypeStruct
    swap = [(0, 1), (1, 0)]
    scale = float(cells * n_lon) ** (-0.5)
    n = cells // BLK
    time = ("z", "co")

    spread, tail, head, piece, own_blocks = call(
        entry_kernel,
        [
            shape((steps, 16, BLK), f32),
            shape((BLK, half + BLK), bf16),
            shape((BLK, half + BLK), bf16),
            shape((cells // 2, half), bf16),
            shape((NB, BLK, BLK), bf16),
        ],
        [HBM] * 6,
        [
            pltpu.VMEM(innovations.shape, f32),
            pltpu.VMEM(obs_cell.shape, i32),
            pltpu.SMEM(tangent_order.shape, i32),
            pltpu.VMEM((2, BLK, half), bf16),
            pltpu.VMEM((2, BLK, BLK), bf16),
            pltpu.VMEM((NB, BLK, BLK), f32),
            pltpu.SemaphoreType.DMA((9,)),
        ],
        flops=10**7,
        data=10**6,
    )(innovations, obs_cell, tangent_order, anomalies, localization, tangent_blocks.reshape(NB, BLK, BLK))

    upward, downward = [], []
    for c in range(2):
        for k in range(n_lon):
            for e in range(2):
                f = e if c == 0 else 1 - e
                k2 = (k + 1) % n_lon
                upward.append(((c * n_lon + k) * 2 + e, (c * n_lon + k2) * 2 + f))
                downward.append(((c * n_lon + k2) * 2 + e, (c * n_lon + k) * 2 + f))
    up0 = lax.ppermute(tail, ("co", "lon", "ens"), upward)
    down0 = lax.ppermute(head, ("co", "lon", "ens"), downward)
    near = lax.ppermute(piece, "ens", swap)
    recv = lax.all_to_all(spread, time, 0, 0, tiled=True)
    oth_blocks = lax.ppermute(own_blocks, "co", swap)
    count = nz + 1
    traj, *sends = call(
        choose_kernel,
        [shape((steps + 1, NB), i32)] + [shape((2, BLK, BLK), bf16)] * (nz // 2) + [shape((BLK, BLK), bf16)],
        [HBM, HBM, VM],
        [
            pltpu.VMEM((steps, BLK), i32),
            pltpu.SMEM((steps, BLK), i32),
            pltpu.VMEM((nz // 2 + 1, BLK, BLK), f32),
            pltpu.SemaphoreType.DMA((count + 1,)),
        ],
        flops=10**6,
        data=10**6,
        specs=[SM] + [VM] * (nz // 2 + 1),
    )(tangent_blocks.reshape(NB, BLK, BLK), oth_blocks, recv)
    got = []
    for d in range(1, nz // 2):
        pairs = []
        for k in range(nz):
            pairs.append((2 * k, (k + d) % nz * 2))
            pairs.append((2 * k + 1, (k - d) % nz * 2 + 1))
        got.append(lax.ppermute(sends[d], time, pairs))
    last = lax.ppermute(sends[nz // 2], "z", [(k, (k + nz // 2) % nz) for k in range(nz)])
    crossed = []
    for g in got + [last]:
        crossed.append(lax.ppermute(g, "co", swap))
    held = [sends[0], *got, sends[0], *crossed[:-1], last, crossed[-1]]

    up1 = lax.ppermute(up0, "co", swap)
    down1 = lax.ppermute(down0, "co", swap)
    lt, gown, asel, ends = call(
        ready_kernel,
        [
            shape((n, BLK, 3 * BLK), bf16),
            shape((cells, half), bf16),
            shape((half // 2, cells), bf16),
            shape((2, BLK, half), bf16),
        ],
        [HBM] * 6,
        [
            pltpu.VMEM(anomalies.shape, bf16),
            pltpu.VMEM(localization.shape, bf16),
            pltpu.VMEM((4, BLK, half + BLK), bf16),
            pltpu.VMEM((cells + 2 * BLK, half), bf16),
            pltpu.SemaphoreType.DMA((6,)),
        ],
        flops=10**9,
        data=4 * 10**6,
    )(anomalies, localization, up0, up1, down0, down1)
    far = lax.ppermute(near, "co", swap)
    (prod,) = call(
        functools.partial(product_kernel, scale),
        [shape((half // 2, steps * BLK), bf16)],
        [HBM, HBM, VM, VM, VM, VM, VM],
        [
            pltpu.VMEM((cells + 2 * BLK, half), bf16),
            pltpu.VMEM((cells, COLS), bf16),
            pltpu.VMEM((cells, steps * BLK), bf16),
            pltpu.VMEM((cells, BLK), f32),
            pltpu.VMEM((half // 2, steps * BLK), bf16),
            pltpu.VMEM((steps, BLK), i32),
            pltpu.SMEM((steps, BLK), i32),
            pltpu.SemaphoreType.DMA((4,)),
            pltpu.SemaphoreType.DMA((4,)),
        ],
        flops=10**9,
        data=4 * 10**6,
        grant=24,
        specs=[HBM],
    )(near, far, ends, lt, gown, asel, recv)
    rows = half // 2 // n_lon
    parts = lax.all_to_all(prod, "lon", 0, 0, tiled=True).reshape(n_lon, rows, steps * BLK)
    (states,) = call(
        scan_kernel,
        [shape((steps, 2, rows, BLK), bf16)],
        [VM] * (1 + len(held)),
        [pltpu.VMEM((steps, BLK, BLK), bf16)],
        flops=10**9,
        data=2 * 10**6,
    )(parts, *held)
    back = lax.all_to_all(states, time, 0, 0, tiled=True)
    x, y = call(place_kernel, [shape((1, 2 * rows, COLS), f32)] * 2, [VM, SM], flops=10**6, data=10**6)(back, traj)
    return x, y


def solution(mesh):
    tm, lon, ens = (mesh.shape[a] for a in ("tm", "lon", "ens"))
    fine = Mesh(mesh.devices.reshape(tm // 2, 2, lon, ens), ("z", "co", "lon", "ens"))
    time = ("z", "co")
    placed = (
        P("lon", "ens"),
        P("lon", None, None, None),
        P(time, "lon"),
        P(time, "lon"),
        P(time, None, None, None),
        P(time, None),
    )
    outs = P(time, ("ens", "lon"), None)

    return jax.shard_map(on_device, mesh=fine, in_specs=placed, out_specs=(outs, outs), check_vma=False)
```

```python
import functools

import jax
import jax.numpy as jnp
from jax import lax
from jax.experimental import pallas as pl
from jax.experimental.pallas import tpu as pltpu
from jax.sharding import Mesh
from jax.sharding import PartitionSpec as P

BLK = 128
NB = 8
COLS = NB * BLK
bf16 = jnp.bfloat16
f32 = jnp.float32
i32 = jnp.int32

VM = pl.BlockSpec(memory_space=pltpu.VMEM)
SM = pl.BlockSpec(memory_space=pltpu.SMEM)
HBM = pl.BlockSpec(memory_space=pltpu.HBM)
MIB = 1024 * 1024
NT = (((1,), (1,)), ((), ()))


def call(kernel, outs, ins, scratch=(), flops=0, data=0, grant=16, specs=None):
    made = pl.pallas_call(
        kernel,
        out_shape=outs,
        in_specs=ins,
        out_specs=specs or [VM] * len(outs),
        scratch_shapes=list(scratch),
        compiler_params=pltpu.CompilerParams(vmem_limit_bytes=grant * MIB),
        cost_estimate=pl.CostEstimate(flops=flops, bytes_accessed=data, transcendentals=0),
    )

    def run(*args):
        args = [pltpu.with_memory_space_constraint(a, pltpu.HBM) if i is HBM else a for a, i in zip(args, ins)]
        return made(*args)

    return run


def cols_at(i):
    return pl.ds(pl.multiple_of(i * BLK, BLK), BLK)


def rows_at(i, n):
    return pl.ds(pl.multiple_of(i * n, n), n)


def copies_of(pairs, sem):
    out = [pltpu.make_async_copy(a, b, sem.at[i]) for i, (a, b) in enumerate(pairs)]
    for c in out:
        c.start()
    return out


def entry_kernel(
    innov, cell, order, anom, loc, tang, spread, up, down, piece, own, innov_v, cell_v, order_s, edge, ends, tang_v, sem
):
    co = lax.axis_index("co")
    cells = anom.shape[0]
    n = loc.shape[0]
    h = piece.shape[0]
    copies = copies_of(
        (
            (innov, innov_v),
            (cell, cell_v),
            (order, order_s),
            (anom.at[pl.ds(cells - BLK, BLK)], edge.at[0]),
            (anom.at[pl.ds(0, BLK)], edge.at[1]),
            (loc.at[n - 1, 2], ends.at[0]),
            (loc.at[0, 0], ends.at[1]),
            (anom.at[rows_at(co, h)], piece),
            (tang, tang_v),
        ),
        sem,
    )
    for c in copies[:3]:
        c.wait()
    x = innov_v[...]
    hi = x.astype(bf16)
    mid = (x - hi.astype(f32)).astype(bf16)
    lo = (x - hi.astype(f32) - mid.astype(f32)).astype(bf16)
    rows = jnp.concatenate([hi, mid, lo, jnp.zeros((5, x.shape[1]), bf16)], axis=0)
    ids = lax.broadcasted_iota(i32, (cells, 1), 0)
    hit = jnp.where(ids == cell_v[...], 1.0, 0.0).astype(bf16)
    y = lax.dot_general(rows, hit, NT, preferred_element_type=f32)
    w = y[0:1] + y[1:2] + y[2:3]
    lane = lax.broadcasted_iota(i32, (8, BLK), 1)
    tag = jnp.zeros((8, BLK), f32)
    for i in range(NB):
        tag = jnp.where(lane == i, order_s[0, i].astype(f32), tag)
    one = jnp.concatenate([w[:, i * BLK : (i + 1) * BLK] for i in range(cells // BLK)] + [tag], axis=0)
    for k in range(spread.shape[0]):
        spread[k] = one
    for c in copies[3:]:
        c.wait()
    half = edge.shape[2]
    for j, out in enumerate((up, down)):
        out[:, :half] = edge[j]
        out[:, half:] = ends[j]
    own[...] = tang_v[...].astype(bf16)


def choose_kernel(own, oth, recv, traj, *refs):
    *outs, ints, order_s, picked, sem = refs
    z = lax.axis_index("z")
    co = lax.axis_index("co")
    steps = recv.shape[0]
    nz = steps // 2
    for k in range(steps):
        ints[k : k + 1] = recv[k, 8:9, :].astype(i32)
    d = pltpu.make_async_copy(ints, order_s, sem.at[0])
    d.start()
    d.wait()
    at = [jnp.int32(q) for q in range(NB)]
    for t in range(steps - 1, -1, -1):
        for q in range(NB):
            traj[t + 1, q] = at[q]
        at = [order_s[t, b] for b in at]
    for q in range(NB):
        traj[0, q] = at[q]
    copies = []
    for d, out in enumerate(outs):
        q = lax.rem(jnp.where(co == 0, z + d, z + nz - d), nz)
        copies.append((own.at[traj[2 * z + co + 1, q]], picked.at[d]))
        if d < nz // 2:
            copies.append((oth.at[traj[2 * z + 2 - co, q]], out.at[1 - co]))
    for c in copies_of(copies, sem.at[pl.ds(1, len(copies))]):
        c.wait()
    for d, out in enumerate(outs):
        if d < nz // 2:
            out[co] = picked[d].astype(bf16)
        else:
            out[...] = picked[d].astype(bf16)


def ready_kernel(anom, loc, *refs):
    *edges, lt, gown, asel, ends, anom_v, loc_v, edge_v, pad, sem = refs
    co = lax.axis_index("co")
    pairs = [(a, edge_v.at[i]) for i, a in enumerate(edges)]
    copies = copies_of(((loc, loc_v), (anom, anom_v), *pairs), sem)
    n = loc.shape[0]
    half = anom.shape[1]
    for c in copies[2:]:
        c.wait()
    up0, up1, down0, down1 = (edge_v.at[i] for i in range(4))
    before = jnp.where(co == 0, up0[:, :half], up1[:, :half])
    after = jnp.where(co == 0, down0[:, :half], down1[:, :half])
    ends[0] = jnp.where(co == 0, up1[:, :half], up0[:, :half])
    ends[1] = jnp.where(co == 0, down1[:, :half], down0[:, :half])
    copies[0].wait()
    for b in range(n):
        prev = up0[:, half:] if b == 0 else loc_v[b - 1, 2]
        nxt = down0[:, half:] if b == n - 1 else loc_v[b + 1, 0]
        lt[b] = jnp.concatenate([prev.T, loc_v[b, 1].T, nxt.T], axis=1)
    copies[1].wait()
    pad[:BLK] = before
    pad[BLK : BLK + n * BLK] = anom_v[...]
    pad[BLK + n * BLK :] = after
    for b in range(n):
        y = jnp.dot(lt[b], pad[b * BLK : (b + 3) * BLK], preferred_element_type=f32)
        gown[b * BLK : (b + 1) * BLK] = y.astype(bf16)
    at = anom_v[...].T
    for k in range(half // 64):
        asel[k * 32 : (k + 1) * 32] = jnp.where(co == 0, at[k * 64 : k * 64 + 32], at[k * 64 + 32 : (k + 1) * 64])


def product_kernel(
    scale, near, far, ends, lt, gown, asel, recv, out, pad, full, vals, wt, res, ints, order_s, sem, out_sem
):
    co = lax.axis_index("co")
    e = lax.axis_index("ens")
    z = lax.axis_index("z")
    steps = recv.shape[0]
    for k in range(steps):
        ints[k : k + 1] = recv[k, 8:9, :].astype(i32)
    h, half = near.shape
    n = lt.shape[0]
    there = pl.ds(pl.multiple_of((1 - e) * half, half), half)
    copies = copies_of(
        (
            (near, pad.at[pl.ds(pl.multiple_of(BLK + co * h, BLK), h)]),
            (far, pad.at[pl.ds(pl.multiple_of(BLK + (1 - co) * h, BLK), h)]),
            (ints, order_s),
            (gown, full.at[:, pl.ds(pl.multiple_of(e * half, half), half)]),
        ),
        sem,
    )
    blank = jnp.zeros((BLK - steps, BLK), f32)
    for b in range(n):
        wt[b * BLK : (b + 1) * BLK] = jnp.concatenate([recv[:, b, :], blank], axis=0).T
    pad[:BLK] = ends[0]
    pad[BLK + n * BLK :] = ends[1]
    copies[0].wait()
    copies[1].wait()
    for b in range(n):
        y = jnp.dot(lt[b], pad[b * BLK : (b + 3) * BLK], preferred_element_type=f32)
        full[b * BLK : (b + 1) * BLK, there] = y.astype(bf16)
    copies[2].wait()
    copies[3].wait()
    at = [None] * steps
    b = z
    for t in range(steps - 1, -1, -1):
        at[t] = cols_at(b)
        b = order_s[t, b]
    for t in range(steps):
        w = jnp.broadcast_to(wt[:, t : t + 1], (n * BLK, BLK)).astype(bf16)
        vals[:, t * BLK : (t + 1) * BLK] = w * full[:, at[t]]
    sent = []
    width = steps * BLK // out_sem.shape[0]
    for g in range(out_sem.shape[0]):
        cols = slice(g * width, (g + 1) * width)
        y = jnp.dot(asel[...], vals[:, cols], preferred_element_type=f32)
        res[:, cols] = (y * scale).astype(bf16)
        c = pltpu.make_async_copy(res.at[:, cols], out.at[:, cols], out_sem.at[g])
        c.start()
        sent.append(c)
    for c in sent:
        c.wait()


def split(x):
    hi = x.astype(bf16)
    lo = (x - hi.astype(f32)).astype(bf16)
    return jnp.concatenate([hi, lo], axis=0)


def times(x, block, transposed):
    dims = NT if transposed else (((1,), (0,)), ((), ()))
    y = lax.dot_general(split(x), block, dims, preferred_element_type=f32)
    rows = x.shape[0]
    return y[:rows] + y[rows:]


def pack_kernel(*refs):
    *got, out = refs
    for j, src in enumerate(got[:-1]):
        out[2 * j : 2 * j + 2] = src[...]
    out[2 * len(got) - 2] = got[-1][...]


def scan_kernel(parts, own, mine, theirs, out, blocks):
    co = lax.axis_index("co")
    z = lax.axis_index("z")
    n = parts.shape[0]
    steps = parts.shape[2] // BLK
    nz = steps // 2
    h = nz // 2
    blocks[pl.ds(2 * z, 2)] = own[...]
    for d in range(1, h):
        for src, back in ((mine, co == 0), (theirs, co == 1)):
            k = lax.rem(jnp.where(back, z + nz - d, z + d), nz)
            blocks[pl.ds(2 * k, 2)] = src[2 * d - 2 : 2 * d]
    k = lax.rem(z + h, nz)
    blocks[2 * k + co] = mine[2 * h - 2]
    blocks[2 * k + 1 - co] = theirs[2 * h - 2]
    force = []
    for t in range(steps):
        at = slice(t * BLK, (t + 1) * BLK)
        y = parts[0, :, at].astype(f32)
        for s in range(1, n):
            y = y + parts[s, :, at].astype(f32)
        force.append(y)
    x = force[0]
    y = times(force[steps - 1], blocks[steps - 1], False)
    out[0, 0] = x.astype(bf16)
    out[steps - 1, 1] = y.astype(bf16)
    for k in range(1, steps):
        t = steps - 1 - k
        x = times(x, blocks[k], True) + force[k]
        y = times(y + force[t], blocks[t], False)
        out[k, 0] = x.astype(bf16)
        out[t, 1] = y.astype(bf16)


def place_kernel(recv, traj, x, y, xs, ys, sem):
    t = 2 * lax.axis_index("z") + lax.axis_index("co")
    rows = recv.shape[2]
    sent = []
    for j, (to, held) in enumerate(((x, xs), (y, ys))):
        for q in range(NB):
            at = cols_at(traj[t + 1 - j, q])
            for c in range(2):
                held[0, c * rows : (c + 1) * rows, at] = recv[2 * q + c, j].astype(f32)
        c = pltpu.make_async_copy(held, to, sem.at[j])
        c.start()
        sent.append(c)
    for c in sent:
        c.wait()


def on_device(anomalies, localization, innovations, obs_cell, tangent_blocks, tangent_order):
    cells, half = anomalies.shape
    n_lon = lax.axis_size("lon")
    nz = lax.axis_size("z")
    steps = 2 * nz
    shape = jax.ShapeDtypeStruct
    swap = [(0, 1), (1, 0)]
    scale = float(cells * n_lon) ** (-0.5)
    n = cells // BLK
    time = ("z", "co")

    spread, tail, head, piece, own_blocks = call(
        entry_kernel,
        [
            shape((steps, 16, BLK), f32),
            shape((BLK, half + BLK), bf16),
            shape((BLK, half + BLK), bf16),
            shape((cells // 2, half), bf16),
            shape((NB, BLK, BLK), bf16),
        ],
        [HBM] * 6,
        [
            pltpu.VMEM(innovations.shape, f32),
            pltpu.VMEM(obs_cell.shape, i32),
            pltpu.SMEM(tangent_order.shape, i32),
            pltpu.VMEM((2, BLK, half), bf16),
            pltpu.VMEM((2, BLK, BLK), bf16),
            pltpu.VMEM((NB, BLK, BLK), f32),
            pltpu.SemaphoreType.DMA((9,)),
        ],
        flops=10**7,
        data=10**6,
    )(innovations, obs_cell, tangent_order, anomalies, localization, tangent_blocks.reshape(NB, BLK, BLK))

    upward, downward = [], []
    for c in range(2):
        for k in range(n_lon):
            for e in range(2):
                f = e if c == 0 else 1 - e
                k2 = (k + 1) % n_lon
                upward.append(((c * n_lon + k) * 2 + e, (c * n_lon + k2) * 2 + f))
                downward.append(((c * n_lon + k2) * 2 + e, (c * n_lon + k) * 2 + f))
    up0 = lax.ppermute(tail, ("co", "lon", "ens"), upward)
    down0 = lax.ppermute(head, ("co", "lon", "ens"), downward)
    near = lax.ppermute(piece, "ens", swap)
    recv = lax.all_to_all(spread, time, 0, 0, tiled=True)
    oth_blocks = lax.ppermute(own_blocks, "co", swap)
    count = nz + 1
    traj, *sends = call(
        choose_kernel,
        [shape((steps + 1, NB), i32)] + [shape((2, BLK, BLK), bf16)] * (nz // 2) + [shape((BLK, BLK), bf16)],
        [HBM, HBM, VM],
        [
            pltpu.VMEM((steps, BLK), i32),
            pltpu.SMEM((steps, BLK), i32),
            pltpu.VMEM((nz // 2 + 1, BLK, BLK), f32),
            pltpu.SemaphoreType.DMA((count + 1,)),
        ],
        flops=10**6,
        data=10**6,
        specs=[SM] + [VM] * (nz // 2 + 1),
    )(tangent_blocks.reshape(NB, BLK, BLK), oth_blocks, recv)
    got = []
    for d in range(1, nz // 2):
        pairs = []
        for k in range(nz):
            pairs.append((2 * k, (k + d) % nz * 2))
            pairs.append((2 * k + 1, (k - d) % nz * 2 + 1))
        got.append(lax.ppermute(sends[d], time, pairs))
    last = lax.ppermute(sends[nz // 2], "z", [(k, (k + nz // 2) % nz) for k in range(nz)])
    (mine,) = call(pack_kernel, [shape((nz - 1, BLK, BLK), bf16)], [VM] * (nz // 2), data=10**6)(*got, last)
    theirs = lax.ppermute(mine, "co", swap)

    up1 = lax.ppermute(up0, "co", swap)
    down1 = lax.ppermute(down0, "co", swap)
    lt, gown, asel, ends = call(
        ready_kernel,
        [
            shape((n, BLK, 3 * BLK), bf16),
            shape((cells, half), bf16),
            shape((half // 2, cells), bf16),
            shape((2, BLK, half), bf16),
        ],
        [HBM] * 6,
        [
            pltpu.VMEM(anomalies.shape, bf16),
            pltpu.VMEM(localization.shape, bf16),
            pltpu.VMEM((4, BLK, half + BLK), bf16),
            pltpu.VMEM((cells + 2 * BLK, half), bf16),
            pltpu.SemaphoreType.DMA((6,)),
        ],
        flops=10**9,
        data=4 * 10**6,
    )(anomalies, localization, up0, up1, down0, down1)
    far = lax.ppermute(near, "co", swap)
    (prod,) = call(
        functools.partial(product_kernel, scale),
        [shape((half // 2, steps * BLK), bf16)],
        [HBM, VM, VM, VM, VM, VM, VM],
        [
            pltpu.VMEM((cells + 2 * BLK, half), bf16),
            pltpu.VMEM((cells, COLS), bf16),
            pltpu.VMEM((cells, steps * BLK), bf16),
            pltpu.VMEM((cells, BLK), f32),
            pltpu.VMEM((half // 2, steps * BLK), bf16),
            pltpu.VMEM((steps, BLK), i32),
            pltpu.SMEM((steps, BLK), i32),
            pltpu.SemaphoreType.DMA((4,)),
            pltpu.SemaphoreType.DMA((2,)),
        ],
        flops=10**9,
        data=4 * 10**6,
        grant=14,
        specs=[HBM],
    )(near, far, ends, lt, gown, asel, recv)
    rows = half // 2 // n_lon
    parts = lax.all_to_all(prod, "lon", 0, 0, tiled=True).reshape(n_lon, rows, steps * BLK)
    (states,) = call(
        scan_kernel,
        [shape((steps, 2, rows, BLK), bf16)],
        [VM] * 4,
        [pltpu.VMEM((steps, BLK, BLK), bf16)],
        flops=10**9,
        data=2 * 10**6,
    )(parts, sends[0], mine, theirs)
    back = lax.all_to_all(states, time, 0, 0, tiled=True)
    x, y = call(
        place_kernel,
        [shape((1, 2 * rows, COLS), f32)] * 2,
        [VM, SM],
        [pltpu.VMEM((1, 2 * rows, COLS), f32), pltpu.VMEM((1, 2 * rows, COLS), f32), pltpu.SemaphoreType.DMA((2,))],
        flops=10**6,
        data=10**6,
        specs=[HBM, HBM],
    )(back, traj)
    return x, y


def solution(mesh):
    tm, lon, ens = (mesh.shape[a] for a in ("tm", "lon", "ens"))
    fine = Mesh(mesh.devices.reshape(tm // 2, 2, lon, ens), ("z", "co", "lon", "ens"))
    time = ("z", "co")
    placed = (
        P("lon", "ens"),
        P("lon", None, None, None),
        P(time, "lon"),
        P(time, "lon"),
        P(time, None, None, None),
        P(time, None),
    )
    outs = P(time, ("ens", "lon"), None)

    return jax.shard_map(on_device, mesh=fine, in_specs=placed, out_specs=(outs, outs), check_vma=False)
```

```python
import functools

import jax
import jax.numpy as jnp
from jax import lax
from jax.experimental import pallas as pl
from jax.experimental.pallas import tpu as pltpu
from jax.sharding import Mesh
from jax.sharding import PartitionSpec as P

BLK = 128
NB = 8
COLS = NB * BLK
bf16 = jnp.bfloat16
f32 = jnp.float32
i32 = jnp.int32

VM = pl.BlockSpec(memory_space=pltpu.VMEM)
SM = pl.BlockSpec(memory_space=pltpu.SMEM)
HBM = pl.BlockSpec(memory_space=pltpu.HBM)
MIB = 1024 * 1024
NT = (((1,), (1,)), ((), ()))


def call(kernel, outs, ins, scratch=(), flops=0, data=0, grant=16, specs=None):
    made = pl.pallas_call(
        kernel,
        out_shape=outs,
        in_specs=ins,
        out_specs=specs or [VM] * len(outs),
        scratch_shapes=list(scratch),
        compiler_params=pltpu.CompilerParams(vmem_limit_bytes=grant * MIB),
        cost_estimate=pl.CostEstimate(flops=flops, bytes_accessed=data, transcendentals=0),
    )

    def run(*args):
        args = [pltpu.with_memory_space_constraint(a, pltpu.HBM) if i is HBM else a for a, i in zip(args, ins)]
        return made(*args)

    return run


def cols_at(i):
    return pl.ds(pl.multiple_of(i * BLK, BLK), BLK)


def rows_at(i, n):
    return pl.ds(pl.multiple_of(i * n, n), n)


def copies_of(pairs, sem):
    out = [pltpu.make_async_copy(a, b, sem.at[i]) for i, (a, b) in enumerate(pairs)]
    for c in out:
        c.start()
    return out


def entry_kernel(
    innov, cell, order, anom, loc, tang, spread, up, down, piece, own, innov_v, cell_v, order_s, edge, ends, tang_v, sem
):
    co = lax.axis_index("co")
    cells = anom.shape[0]
    n = loc.shape[0]
    h = piece.shape[0]
    copies = copies_of(
        (
            (innov, innov_v),
            (cell, cell_v),
            (order, order_s),
            (anom.at[pl.ds(cells - BLK, BLK)], edge.at[0]),
            (anom.at[pl.ds(0, BLK)], edge.at[1]),
            (loc.at[n - 1, 2], ends.at[0]),
            (loc.at[0, 0], ends.at[1]),
            (anom.at[rows_at(co, h)], piece),
            (tang, tang_v),
        ),
        sem,
    )
    for c in copies[:3]:
        c.wait()
    x = innov_v[...]
    hi = x.astype(bf16)
    mid = (x - hi.astype(f32)).astype(bf16)
    lo = (x - hi.astype(f32) - mid.astype(f32)).astype(bf16)
    rows = jnp.concatenate([hi, mid, lo, jnp.zeros((5, x.shape[1]), bf16)], axis=0)
    ids = lax.broadcasted_iota(i32, (cells, 1), 0)
    hit = jnp.where(ids == cell_v[...], 1.0, 0.0).astype(bf16)
    y = lax.dot_general(rows, hit, NT, preferred_element_type=f32)
    w = y[0:1] + y[1:2] + y[2:3]
    lane = lax.broadcasted_iota(i32, (8, BLK), 1)
    tag = jnp.zeros((8, BLK), f32)
    for i in range(NB):
        tag = jnp.where(lane == i, order_s[0, i].astype(f32), tag)
    one = jnp.concatenate([w[:, i * BLK : (i + 1) * BLK] for i in range(cells // BLK)] + [tag], axis=0)
    for k in range(spread.shape[0]):
        spread[k] = one
    for c in copies[3:]:
        c.wait()
    half = edge.shape[2]
    for j, out in enumerate((up, down)):
        out[:, :half] = edge[j]
        out[:, half:] = ends[j]
    own[...] = tang_v[...].astype(bf16)


def choose_kernel(own, oth, recv, traj, *refs):
    *outs, ints, order_s, sem = refs
    z = lax.axis_index("z")
    co = lax.axis_index("co")
    steps = recv.shape[0]
    nz = steps // 2
    for k in range(steps):
        ints[k : k + 1] = recv[k, 8:9, :].astype(i32)
    d = pltpu.make_async_copy(ints, order_s, sem)
    d.start()
    d.wait()
    at = [jnp.int32(q) for q in range(NB)]
    for t in range(steps - 1, -1, -1):
        for q in range(NB):
            traj[t + 1, q] = at[q]
        at = [order_s[t, b] for b in at]
    for q in range(NB):
        traj[0, q] = at[q]
    for d, out in enumerate(outs):
        q = lax.rem(jnp.where(co == 0, z + d, z + nz - d), nz)
        mine = own[traj[2 * z + co + 1, q]]
        if d < nz // 2:
            out[co] = mine
            out[1 - co] = oth[traj[2 * z + 2 - co, q]]
        else:
            out[...] = mine


def ready_kernel(anom, loc, up0, up1, down0, down1, lt, gown, asel, ends, anom_v, loc_v, pad, held, sem, out_sem):
    co = lax.axis_index("co")
    copies = copies_of(((loc, loc_v), (anom, anom_v)), sem)
    n = loc.shape[0]
    half = anom.shape[1]
    pad[:BLK] = jnp.where(co == 0, up0[:, :half], up1[:, :half])
    pad[BLK + n * BLK :] = jnp.where(co == 0, down0[:, :half], down1[:, :half])
    ends[0] = jnp.where(co == 0, up1[:, :half], up0[:, :half])
    ends[1] = jnp.where(co == 0, down1[:, :half], down0[:, :half])
    copies[0].wait()
    for b in range(n):
        prev = up0[:, half:] if b == 0 else loc_v[b - 1, 2]
        nxt = down0[:, half:] if b == n - 1 else loc_v[b + 1, 0]
        lt[b] = jnp.concatenate([prev.T, loc_v[b, 1].T, nxt.T], axis=1)
    copies[1].wait()
    pad[BLK : BLK + n * BLK] = anom_v[...]
    for b in range(n):
        y = jnp.dot(lt[b], pad[b * BLK : (b + 3) * BLK], preferred_element_type=f32)
        held[b * BLK : (b + 1) * BLK] = y.astype(bf16)
    sent = pltpu.make_async_copy(held, gown, out_sem)
    sent.start()
    at = anom_v[...].T
    for k in range(half // 64):
        asel[k * 32 : (k + 1) * 32] = jnp.where(co == 0, at[k * 64 : k * 64 + 32], at[k * 64 + 32 : (k + 1) * 64])
    sent.wait()


def product_kernel(
    scale, near, far, ends, lt, gown, asel, recv, out, pad, full, vals, wt, res, ints, order_s, sem, out_sem
):
    co = lax.axis_index("co")
    e = lax.axis_index("ens")
    z = lax.axis_index("z")
    steps = recv.shape[0]
    for k in range(steps):
        ints[k : k + 1] = recv[k, 8:9, :].astype(i32)
    h, half = near.shape
    n = lt.shape[0]
    there = pl.ds(pl.multiple_of((1 - e) * half, half), half)
    copies = copies_of(
        (
            (near, pad.at[pl.ds(pl.multiple_of(BLK + co * h, BLK), h)]),
            (far, pad.at[pl.ds(pl.multiple_of(BLK + (1 - co) * h, BLK), h)]),
            (ints, order_s),
            (gown, full.at[:, pl.ds(pl.multiple_of(e * half, half), half)]),
        ),
        sem,
    )
    blank = jnp.zeros((BLK - steps, BLK), f32)
    for b in range(n):
        wt[b * BLK : (b + 1) * BLK] = jnp.concatenate([recv[:, b, :], blank], axis=0).T
    pad[:BLK] = ends[0]
    pad[BLK + n * BLK :] = ends[1]
    copies[0].wait()
    copies[1].wait()
    for b in range(n):
        y = jnp.dot(lt[b], pad[b * BLK : (b + 3) * BLK], preferred_element_type=f32)
        full[b * BLK : (b + 1) * BLK, there] = y.astype(bf16)
    copies[2].wait()
    copies[3].wait()
    at = [None] * steps
    b = z
    for t in range(steps - 1, -1, -1):
        at[t] = cols_at(b)
        b = order_s[t, b]
    for t in range(steps):
        w = jnp.broadcast_to(wt[:, t : t + 1], (n * BLK, BLK)).astype(bf16)
        vals[:, t * BLK : (t + 1) * BLK] = w * full[:, at[t]]
    sent = []
    width = steps * BLK // out_sem.shape[0]
    for g in range(out_sem.shape[0]):
        cols = slice(g * width, (g + 1) * width)
        y = jnp.dot(asel[...], vals[:, cols], preferred_element_type=f32)
        res[:, cols] = (y * scale).astype(bf16)
        c = pltpu.make_async_copy(res.at[:, cols], out.at[:, cols], out_sem.at[g])
        c.start()
        sent.append(c)
    for c in sent:
        c.wait()


def split(x):
    hi = x.astype(bf16)
    lo = (x - hi.astype(f32)).astype(bf16)
    return jnp.concatenate([hi, lo], axis=0)


def times(x, block, transposed):
    dims = NT if transposed else (((1,), (0,)), ((), ()))
    y = lax.dot_general(split(x), block, dims, preferred_element_type=f32)
    rows = x.shape[0]
    return y[:rows] + y[rows:]


def pack_kernel(*refs):
    *got, out = refs
    for j, src in enumerate(got[:-1]):
        out[2 * j : 2 * j + 2] = src[...]
    out[2 * len(got) - 2] = got[-1][...]


def scan_kernel(parts, own, mine, theirs, out, blocks):
    co = lax.axis_index("co")
    z = lax.axis_index("z")
    n = parts.shape[0]
    steps = parts.shape[2] // BLK
    nz = steps // 2
    h = nz // 2
    blocks[pl.ds(2 * z, 2)] = own[...]
    for d in range(1, h):
        for src, back in ((mine, co == 0), (theirs, co == 1)):
            k = lax.rem(jnp.where(back, z + nz - d, z + d), nz)
            blocks[pl.ds(2 * k, 2)] = src[2 * d - 2 : 2 * d]
    k = lax.rem(z + h, nz)
    blocks[2 * k + co] = mine[2 * h - 2]
    blocks[2 * k + 1 - co] = theirs[2 * h - 2]
    force = []
    for t in range(steps):
        at = slice(t * BLK, (t + 1) * BLK)
        y = parts[0, :, at].astype(f32)
        for s in range(1, n):
            y = y + parts[s, :, at].astype(f32)
        force.append(y)
    x = force[0]
    y = times(force[steps - 1], blocks[steps - 1], False)
    out[0, 0] = x.astype(bf16)
    out[steps - 1, 1] = y.astype(bf16)
    for k in range(1, steps):
        t = steps - 1 - k
        x = times(x, blocks[k], True) + force[k]
        y = times(y + force[t], blocks[t], False)
        out[k, 0] = x.astype(bf16)
        out[t, 1] = y.astype(bf16)


def place_kernel(recv, traj, x, y, xs, ys, sem):
    t = 2 * lax.axis_index("z") + lax.axis_index("co")
    rows = recv.shape[2]
    sent = []
    for j, (to, held) in enumerate(((x, xs), (y, ys))):
        for q in range(NB):
            at = cols_at(traj[t + 1 - j, q])
            for c in range(2):
                held[0, c * rows : (c + 1) * rows, at] = recv[2 * q + c, j].astype(f32)
        c = pltpu.make_async_copy(held, to, sem.at[j])
        c.start()
        sent.append(c)
    for c in sent:
        c.wait()


def on_device(anomalies, localization, innovations, obs_cell, tangent_blocks, tangent_order):
    cells, half = anomalies.shape
    n_lon = lax.axis_size("lon")
    nz = lax.axis_size("z")
    steps = 2 * nz
    shape = jax.ShapeDtypeStruct
    swap = [(0, 1), (1, 0)]
    scale = float(cells * n_lon) ** (-0.5)
    n = cells // BLK
    time = ("z", "co")

    spread, tail, head, piece, own_blocks = call(
        entry_kernel,
        [
            shape((steps, 16, BLK), f32),
            shape((BLK, half + BLK), bf16),
            shape((BLK, half + BLK), bf16),
            shape((cells // 2, half), bf16),
            shape((NB, BLK, BLK), bf16),
        ],
        [HBM] * 6,
        [
            pltpu.VMEM(innovations.shape, f32),
            pltpu.VMEM(obs_cell.shape, i32),
            pltpu.SMEM(tangent_order.shape, i32),
            pltpu.VMEM((2, BLK, half), bf16),
            pltpu.VMEM((2, BLK, BLK), bf16),
            pltpu.VMEM((NB, BLK, BLK), f32),
            pltpu.SemaphoreType.DMA((9,)),
        ],
        flops=10**7,
        data=10**6,
    )(innovations, obs_cell, tangent_order, anomalies, localization, tangent_blocks.reshape(NB, BLK, BLK))

    upward, downward = [], []
    for c in range(2):
        for k in range(n_lon):
            for e in range(2):
                f = e if c == 0 else 1 - e
                k2 = (k + 1) % n_lon
                upward.append(((c * n_lon + k) * 2 + e, (c * n_lon + k2) * 2 + f))
                downward.append(((c * n_lon + k2) * 2 + e, (c * n_lon + k) * 2 + f))
    up0 = lax.ppermute(tail, ("co", "lon", "ens"), upward)
    down0 = lax.ppermute(head, ("co", "lon", "ens"), downward)
    near = lax.ppermute(piece, "ens", swap)
    recv = lax.all_to_all(spread, time, 0, 0, tiled=True)
    oth_blocks = lax.ppermute(own_blocks, "co", swap)
    traj, *sends = call(
        choose_kernel,
        [shape((steps + 1, NB), i32)] + [shape((2, BLK, BLK), bf16)] * (nz // 2) + [shape((BLK, BLK), bf16)],
        [VM] * 3,
        [pltpu.VMEM((steps, BLK), i32), pltpu.SMEM((steps, BLK), i32), pltpu.SemaphoreType.DMA],
        flops=10**6,
        data=10**6,
        specs=[SM] + [VM] * (nz // 2 + 1),
        grant=4,
    )(own_blocks, oth_blocks, recv)
    got = []
    for d in range(1, nz // 2):
        pairs = []
        for k in range(nz):
            pairs.append((2 * k, (k + d) % nz * 2))
            pairs.append((2 * k + 1, (k - d) % nz * 2 + 1))
        got.append(lax.ppermute(sends[d], time, pairs))
    last = lax.ppermute(sends[nz // 2], "z", [(k, (k + nz // 2) % nz) for k in range(nz)])
    (mine,) = call(pack_kernel, [shape((nz - 1, BLK, BLK), bf16)], [VM] * (nz // 2), data=10**6)(*got, last)
    theirs = lax.ppermute(mine, "co", swap)

    up1 = lax.ppermute(up0, "co", swap)
    down1 = lax.ppermute(down0, "co", swap)
    lt, gown, asel, ends = call(
        ready_kernel,
        [
            shape((n, BLK, 3 * BLK), bf16),
            pltpu.HBM((cells, half), bf16),
            shape((half // 2, cells), bf16),
            shape((2, BLK, half), bf16),
        ],
        [HBM, HBM, VM, VM, VM, VM],
        [
            pltpu.VMEM(anomalies.shape, bf16),
            pltpu.VMEM(localization.shape, bf16),
            pltpu.VMEM((cells + 2 * BLK, half), bf16),
            pltpu.VMEM((cells, half), bf16),
            pltpu.SemaphoreType.DMA((2,)),
            pltpu.SemaphoreType.DMA,
        ],
        flops=10**9,
        data=4 * 10**6,
        specs=[VM, HBM, VM, VM],
        grant=10,
    )(anomalies, localization, up0, up1, down0, down1)
    far = lax.ppermute(near, "co", swap)
    (prod,) = call(
        functools.partial(product_kernel, scale),
        [shape((half // 2, steps * BLK), bf16)],
        [HBM, VM, VM, VM, HBM, VM, VM],
        [
            pltpu.VMEM((cells + 2 * BLK, half), bf16),
            pltpu.VMEM((cells, COLS), bf16),
            pltpu.VMEM((cells, steps * BLK), bf16),
            pltpu.VMEM((cells, BLK), f32),
            pltpu.VMEM((half // 2, steps * BLK), bf16),
            pltpu.VMEM((steps, BLK), i32),
            pltpu.SMEM((steps, BLK), i32),
            pltpu.SemaphoreType.DMA((4,)),
            pltpu.SemaphoreType.DMA((2,)),
        ],
        flops=10**9,
        data=4 * 10**6,
        grant=14,
        specs=[HBM],
    )(near, far, ends, lt, gown, asel, recv)
    rows = half // 2 // n_lon
    parts = lax.all_to_all(prod, "lon", 0, 0, tiled=True).reshape(n_lon, rows, steps * BLK)
    (states,) = call(
        scan_kernel,
        [shape((steps, 2, rows, BLK), bf16)],
        [VM] * 4,
        [pltpu.VMEM((steps, BLK, BLK), bf16)],
        flops=10**9,
        data=2 * 10**6,
    )(parts, sends[0], mine, theirs)
    back = lax.all_to_all(states, time, 0, 0, tiled=True)
    x, y = call(
        place_kernel,
        [shape((1, 2 * rows, COLS), f32)] * 2,
        [VM, SM],
        [pltpu.VMEM((1, 2 * rows, COLS), f32), pltpu.VMEM((1, 2 * rows, COLS), f32), pltpu.SemaphoreType.DMA((2,))],
        flops=10**6,
        data=10**6,
        specs=[HBM, HBM],
    )(back, traj)
    return x, y


def solution(mesh):
    tm, lon, ens = (mesh.shape[a] for a in ("tm", "lon", "ens"))
    fine = Mesh(mesh.devices.reshape(tm // 2, 2, lon, ens), ("z", "co", "lon", "ens"))
    time = ("z", "co")
    placed = (
        P("lon", "ens"),
        P("lon", None, None, None),
        P(time, "lon"),
        P(time, "lon"),
        P(time, None, None, None),
        P(time, None),
    )
    outs = P(time, ("ens", "lon"), None)

    return jax.shard_map(on_device, mesh=fine, in_specs=placed, out_specs=(outs, outs), check_vma=False)
```

```python
import functools

import jax
import jax.numpy as jnp
from jax import lax
from jax.experimental import pallas as pl
from jax.experimental.pallas import tpu as pltpu
from jax.sharding import Mesh
from jax.sharding import PartitionSpec as P

BLK = 128
NB = 8
COLS = NB * BLK
bf16 = jnp.bfloat16
f32 = jnp.float32
i32 = jnp.int32

VM = pl.BlockSpec(memory_space=pltpu.VMEM)
SM = pl.BlockSpec(memory_space=pltpu.SMEM)
HBM = pl.BlockSpec(memory_space=pltpu.HBM)
MIB = 1024 * 1024
NT = (((1,), (1,)), ((), ()))


def call(kernel, outs, ins, scratch=(), flops=0, data=0, grant=16, specs=None):
    made = pl.pallas_call(
        kernel,
        out_shape=outs,
        in_specs=ins,
        out_specs=specs or [VM] * len(outs),
        scratch_shapes=list(scratch),
        compiler_params=pltpu.CompilerParams(vmem_limit_bytes=grant * MIB),
        cost_estimate=pl.CostEstimate(flops=flops, bytes_accessed=data, transcendentals=0),
    )

    def run(*args):
        args = [pltpu.with_memory_space_constraint(a, pltpu.HBM) if i is HBM else a for a, i in zip(args, ins)]
        return made(*args)

    return run


def cols_at(i):
    return pl.ds(pl.multiple_of(i * BLK, BLK), BLK)


def copies_of(pairs, sem):
    out = [pltpu.make_async_copy(a, b, sem.at[i]) for i, (a, b) in enumerate(pairs)]
    for c in out:
        c.start()
    return out


def entry_kernel(
    innov, cell, order, anom, loc, tang, spread, up, down, own, innov_v, cell_v, order_s, edge, ends, tang_v, sem
):
    cells = anom.shape[0]
    n = loc.shape[0]
    copies = copies_of(
        (
            (innov, innov_v),
            (cell, cell_v),
            (order, order_s),
            (anom.at[pl.ds(cells - BLK, BLK)], edge.at[0]),
            (anom.at[pl.ds(0, BLK)], edge.at[1]),
            (loc.at[n - 1, 2], ends.at[0]),
            (loc.at[0, 0], ends.at[1]),
            (tang, tang_v),
        ),
        sem,
    )
    for c in copies[:3]:
        c.wait()
    x = innov_v[...]
    hi = x.astype(bf16)
    mid = (x - hi.astype(f32)).astype(bf16)
    lo = (x - hi.astype(f32) - mid.astype(f32)).astype(bf16)
    rows = jnp.concatenate([hi, mid, lo, jnp.zeros((5, x.shape[1]), bf16)], axis=0)
    ids = lax.broadcasted_iota(i32, (cells, 1), 0)
    hit = jnp.where(ids == cell_v[...], 1.0, 0.0).astype(bf16)
    y = lax.dot_general(rows, hit, NT, preferred_element_type=f32)
    w = y[0:1] + y[1:2] + y[2:3]
    lane = lax.broadcasted_iota(i32, (8, BLK), 1)
    tag = jnp.zeros((8, BLK), f32)
    for i in range(NB):
        tag = jnp.where(lane == i, order_s[0, i].astype(f32), tag)
    one = jnp.concatenate([w[:, i * BLK : (i + 1) * BLK] for i in range(cells // BLK)] + [tag], axis=0)
    for k in range(spread.shape[0]):
        spread[k] = one
    for c in copies[3:]:
        c.wait()
    half = edge.shape[2]
    for j, out in enumerate((up, down)):
        out[:, :half] = edge[j]
        out[:, half:] = ends[j]
    own[...] = tang_v[...].astype(bf16)


def choose_kernel(own, oth, recv, traj, *refs):
    *outs, ints, order_s, sem = refs
    z = lax.axis_index("z")
    co = lax.axis_index("co")
    steps = recv.shape[0]
    nz = steps // 2
    for k in range(steps):
        ints[k : k + 1] = recv[k, 8:9, :].astype(i32)
    d = pltpu.make_async_copy(ints, order_s, sem)
    d.start()
    d.wait()
    at = [jnp.int32(q) for q in range(NB)]
    for t in range(steps - 1, -1, -1):
        for q in range(NB):
            traj[t + 1, q] = at[q]
        at = [order_s[t, b] for b in at]
    for q in range(NB):
        traj[0, q] = at[q]
    for d, out in enumerate(outs):
        q = lax.rem(jnp.where(co == 0, z + d, z + nz - d), nz)
        mine = own[traj[2 * z + co + 1, q]]
        if d < nz // 2:
            out[co] = mine
            out[1 - co] = oth[traj[2 * z + 2 - co, q]]
        else:
            out[...] = mine


def ready_kernel(anom, loc, lt, gown, asel, anom_v, loc_v, held, sem, out_sem):
    co = lax.axis_index("co")
    copies = copies_of(((loc, loc_v), (anom, anom_v)), sem)
    n = loc.shape[0]
    half = anom.shape[1]
    none = jnp.zeros((BLK, BLK), bf16)
    copies[0].wait()
    for b in range(n):
        prev = none if b == 0 else loc_v[b - 1, 2].T
        nxt = none if b == n - 1 else loc_v[b + 1, 0].T
        lt[b] = jnp.concatenate([prev, loc_v[b, 1].T, nxt], axis=1)
    copies[1].wait()
    held[:BLK] = jnp.zeros((BLK, half), bf16)
    held[(n - 1) * BLK :] = jnp.zeros((BLK, half), bf16)
    for b in range(1, n - 1):
        y = jnp.dot(lt[b], anom_v[(b - 1) * BLK : (b + 2) * BLK], preferred_element_type=f32)
        held[b * BLK : (b + 1) * BLK] = y.astype(bf16)
    sent = pltpu.make_async_copy(held, gown, out_sem)
    sent.start()
    at = anom_v[...].T
    for k in range(half // 64):
        asel[k * 32 : (k + 1) * 32] = jnp.where(co == 0, at[k * 64 : k * 64 + 32], at[k * 64 + 32 : (k + 1) * 64])
    sent.wait()


def product_kernel(
    scale,
    fetched,
    handed,
    anom,
    gown,
    up0,
    up1,
    down0,
    down1,
    lt,
    asel,
    recv,
    out,
    pad,
    full,
    vals,
    wt,
    res,
    ends,
    ints,
    order_s,
    sem,
    out_sem,
):
    co = lax.axis_index("co")
    e = lax.axis_index("ens")
    z = lax.axis_index("z")
    steps = recv.shape[0]
    for k in range(steps):
        ints[k : k + 1] = recv[k, 8:9, :].astype(i32)
    cells, half = anom.shape
    n = lt.shape[0]
    here = pl.ds(pl.multiple_of(e * half, half), half)
    there = pl.ds(pl.multiple_of((1 - e) * half, half), half)

    def other(src):
        return pltpu.make_async_copy(src, pad.at[pl.ds(BLK, cells)], sem.at[0])

    @pl.when(co == e)
    def _():
        other(handed).start()

    @pl.when(co != e)
    def _():
        other(fetched).start()

    copies = copies_of(
        (
            (anom.at[pl.ds(0, 2 * BLK)], ends.at[0]),
            (ints, order_s),
            (gown, full.at[:, here]),
            (anom.at[pl.ds(cells - 2 * BLK, 2 * BLK)], ends.at[1]),
        ),
        sem.at[pl.ds(1, 4)],
    )
    blank = jnp.zeros((BLK - steps, BLK), f32)
    for b in range(n):
        wt[b * BLK : (b + 1) * BLK] = jnp.concatenate([recv[:, b, :], blank], axis=0).T
    first = jnp.concatenate([up0[:, half:].T, lt[0, :, BLK:]], axis=1)
    final = jnp.concatenate([lt[n - 1, :, : 2 * BLK], down0[:, half:].T], axis=1)
    pad[:BLK] = jnp.where(co == 0, up1[:, :half], up0[:, :half])
    pad[BLK + cells :] = jnp.where(co == 0, down1[:, :half], down0[:, :half])
    other(fetched).wait()
    for b in range(n):
        left = first if b == 0 else final if b == n - 1 else lt[b]
        y = jnp.dot(left, pad[b * BLK : (b + 3) * BLK], preferred_element_type=f32)
        full[b * BLK : (b + 1) * BLK, there] = y.astype(bf16)
    copies[0].wait()
    copies[3].wait()
    top = jnp.concatenate([jnp.where(co == 0, up0[:, :half], up1[:, :half]), ends[0]], axis=0)
    low = jnp.concatenate([ends[1], jnp.where(co == 0, down0[:, :half], down1[:, :half])], axis=0)
    top = jnp.dot(first, top, preferred_element_type=f32).astype(bf16)
    low = jnp.dot(final, low, preferred_element_type=f32).astype(bf16)
    copies[1].wait()
    copies[2].wait()
    full[:BLK, here] = top
    full[cells - BLK :, here] = low
    at = [None] * steps
    b = z
    for t in range(steps - 1, -1, -1):
        at[t] = cols_at(b)
        b = order_s[t, b]
    for t in range(steps):
        w = jnp.broadcast_to(wt[:, t : t + 1], (n * BLK, BLK)).astype(bf16)
        vals[:, t * BLK : (t + 1) * BLK] = w * full[:, at[t]]
    sent = []
    width = steps * BLK // out_sem.shape[0]
    for g in range(out_sem.shape[0]):
        cols = slice(g * width, (g + 1) * width)
        y = jnp.dot(asel[...], vals[:, cols], preferred_element_type=f32)
        res[:, cols] = (y * scale).astype(bf16)
        c = pltpu.make_async_copy(res.at[:, cols], out.at[:, cols], out_sem.at[g])
        c.start()
        sent.append(c)
    for c in sent:
        c.wait()


def split(x):
    hi = x.astype(bf16)
    lo = (x - hi.astype(f32)).astype(bf16)
    return jnp.concatenate([hi, lo], axis=0)


def times(x, block, transposed):
    dims = NT if transposed else (((1,), (0,)), ((), ()))
    y = lax.dot_general(split(x), block, dims, preferred_element_type=f32)
    rows = x.shape[0]
    return y[:rows] + y[rows:]


def pack_kernel(*refs):
    *got, out = refs
    for j, src in enumerate(got[:-1]):
        out[2 * j : 2 * j + 2] = src[...]
    out[2 * len(got) - 2] = got[-1][...]


def scan_kernel(parts, own, mine, theirs, out, blocks):
    co = lax.axis_index("co")
    z = lax.axis_index("z")
    n = parts.shape[0]
    steps = parts.shape[2] // BLK
    nz = steps // 2
    h = nz // 2
    blocks[pl.ds(2 * z, 2)] = own[...]
    for d in range(1, h):
        for src, back in ((mine, co == 0), (theirs, co == 1)):
            k = lax.rem(jnp.where(back, z + nz - d, z + d), nz)
            blocks[pl.ds(2 * k, 2)] = src[2 * d - 2 : 2 * d]
    k = lax.rem(z + h, nz)
    blocks[2 * k + co] = mine[2 * h - 2]
    blocks[2 * k + 1 - co] = theirs[2 * h - 2]
    force = []
    for t in range(steps):
        at = slice(t * BLK, (t + 1) * BLK)
        y = parts[0, :, at].astype(f32)
        for s in range(1, n):
            y = y + parts[s, :, at].astype(f32)
        force.append(y)
    x = force[0]
    y = times(force[steps - 1], blocks[steps - 1], False)
    out[0, 0] = x.astype(bf16)
    out[steps - 1, 1] = y.astype(bf16)
    for k in range(1, steps):
        t = steps - 1 - k
        x = times(x, blocks[k], True) + force[k]
        y = times(y + force[t], blocks[t], False)
        out[k, 0] = x.astype(bf16)
        out[t, 1] = y.astype(bf16)


def place_kernel(recv, traj, x, y, xs, ys, sem):
    t = 2 * lax.axis_index("z") + lax.axis_index("co")
    rows = recv.shape[2]
    sent = []
    for j, (to, held) in enumerate(((x, xs), (y, ys))):
        for q in range(NB):
            at = cols_at(traj[t + 1 - j, q])
            for c in range(2):
                held[0, c * rows : (c + 1) * rows, at] = recv[2 * q + c, j].astype(f32)
        c = pltpu.make_async_copy(held, to, sem.at[j])
        c.start()
        sent.append(c)
    for c in sent:
        c.wait()


def on_device(anomalies, localization, innovations, obs_cell, tangent_blocks, tangent_order):
    cells, half = anomalies.shape
    n_lon = lax.axis_size("lon")
    nz = lax.axis_size("z")
    steps = 2 * nz
    shape = jax.ShapeDtypeStruct
    swap = [(0, 1), (1, 0)]
    scale = float(cells * n_lon) ** (-0.5)
    n = cells // BLK
    time = ("z", "co")

    spread, tail, head, own_blocks = call(
        entry_kernel,
        [
            shape((steps, 16, BLK), f32),
            shape((BLK, half + BLK), bf16),
            shape((BLK, half + BLK), bf16),
            shape((NB, BLK, BLK), bf16),
        ],
        [HBM] * 6,
        [
            pltpu.VMEM(innovations.shape, f32),
            pltpu.VMEM(obs_cell.shape, i32),
            pltpu.SMEM(tangent_order.shape, i32),
            pltpu.VMEM((2, BLK, half), bf16),
            pltpu.VMEM((2, BLK, BLK), bf16),
            pltpu.VMEM((NB, BLK, BLK), f32),
            pltpu.SemaphoreType.DMA((8,)),
        ],
        flops=10**7,
        data=10**6,
    )(innovations, obs_cell, tangent_order, anomalies, localization, tangent_blocks.reshape(NB, BLK, BLK))

    upward, downward = [], []
    for c in range(2):
        for k in range(n_lon):
            for e in range(2):
                f = e if c == 0 else 1 - e
                k2 = (k + 1) % n_lon
                upward.append(((c * n_lon + k) * 2 + e, (c * n_lon + k2) * 2 + f))
                downward.append(((c * n_lon + k2) * 2 + e, (c * n_lon + k) * 2 + f))
    up0 = lax.ppermute(tail, ("co", "lon", "ens"), upward)
    down0 = lax.ppermute(head, ("co", "lon", "ens"), downward)
    fetched = lax.ppermute(anomalies, ("co", "ens"), [(0, 1), (3, 2)])
    recv = lax.all_to_all(spread, time, 0, 0, tiled=True)
    oth_blocks = lax.ppermute(own_blocks, "co", swap)
    traj, *sends = call(
        choose_kernel,
        [shape((steps + 1, NB), i32)] + [shape((2, BLK, BLK), bf16)] * (nz // 2) + [shape((BLK, BLK), bf16)],
        [VM] * 3,
        [pltpu.VMEM((steps, BLK), i32), pltpu.SMEM((steps, BLK), i32), pltpu.SemaphoreType.DMA],
        flops=10**6,
        data=10**6,
        specs=[SM] + [VM] * (nz // 2 + 1),
        grant=4,
    )(own_blocks, oth_blocks, recv)
    got = []
    for d in range(1, nz // 2):
        pairs = []
        for k in range(nz):
            pairs.append((2 * k, (k + d) % nz * 2))
            pairs.append((2 * k + 1, (k - d) % nz * 2 + 1))
        got.append(lax.ppermute(sends[d], time, pairs))
    last = lax.ppermute(sends[nz // 2], "z", [(k, (k + nz // 2) % nz) for k in range(nz)])
    (mine,) = call(pack_kernel, [shape((nz - 1, BLK, BLK), bf16)], [VM] * (nz // 2), data=10**6)(*got, last)
    theirs = lax.ppermute(mine, "co", swap)

    up1 = lax.ppermute(up0, "co", swap)
    down1 = lax.ppermute(down0, "co", swap)
    lt, gown, asel = call(
        ready_kernel,
        [
            shape((n, BLK, 3 * BLK), bf16),
            pltpu.HBM((cells, half), bf16),
            shape((half // 2, cells), bf16),
        ],
        [HBM, HBM],
        [
            pltpu.VMEM(anomalies.shape, bf16),
            pltpu.VMEM(localization.shape, bf16),
            pltpu.VMEM((cells, half), bf16),
            pltpu.SemaphoreType.DMA((2,)),
            pltpu.SemaphoreType.DMA,
        ],
        flops=10**9,
        data=4 * 10**6,
        specs=[VM, HBM, VM],
        grant=10,
    )(anomalies, localization)
    handed = lax.ppermute(fetched, ("co", "ens"), [(1, 3), (2, 0)])
    (prod,) = call(
        functools.partial(product_kernel, scale),
        [shape((half // 2, steps * BLK), bf16)],
        [HBM] * 4 + [VM] * 7,
        [
            pltpu.VMEM((cells + 2 * BLK, half), bf16),
            pltpu.VMEM((cells, COLS), bf16),
            pltpu.VMEM((cells, steps * BLK), bf16),
            pltpu.VMEM((cells, BLK), f32),
            pltpu.VMEM((half // 2, steps * BLK), bf16),
            pltpu.VMEM((2, 2 * BLK, half), bf16),
            pltpu.VMEM((steps, BLK), i32),
            pltpu.SMEM((steps, BLK), i32),
            pltpu.SemaphoreType.DMA((5,)),
            pltpu.SemaphoreType.DMA((2,)),
        ],
        flops=10**9,
        data=4 * 10**6,
        grant=16,
        specs=[HBM],
    )(fetched, handed, anomalies, gown, up0, up1, down0, down1, lt, asel, recv)
    rows = half // 2 // n_lon
    parts = lax.all_to_all(prod, "lon", 0, 0, tiled=True).reshape(n_lon, rows, steps * BLK)
    (states,) = call(
        scan_kernel,
        [shape((steps, 2, rows, BLK), bf16)],
        [VM] * 4,
        [pltpu.VMEM((steps, BLK, BLK), bf16)],
        flops=10**9,
        data=2 * 10**6,
    )(parts, sends[0], mine, theirs)
    back = lax.all_to_all(states, time, 0, 0, tiled=True)
    x, y = call(
        place_kernel,
        [shape((1, 2 * rows, COLS), f32)] * 2,
        [VM, SM],
        [pltpu.VMEM((1, 2 * rows, COLS), f32), pltpu.VMEM((1, 2 * rows, COLS), f32), pltpu.SemaphoreType.DMA((2,))],
        flops=10**6,
        data=10**6,
        specs=[HBM, HBM],
    )(back, traj)
    return x, y


def solution(mesh):
    tm, lon, ens = (mesh.shape[a] for a in ("tm", "lon", "ens"))
    fine = Mesh(mesh.devices.reshape(tm // 2, 2, lon, ens), ("z", "co", "lon", "ens"))
    time = ("z", "co")
    placed = (
        P("lon", "ens"),
        P("lon", None, None, None),
        P(time, "lon"),
        P(time, "lon"),
        P(time, None, None, None),
        P(time, None),
    )
    outs = P(time, ("ens", "lon"), None)

    return jax.shard_map(on_device, mesh=fine, in_specs=placed, out_specs=(outs, outs), check_vma=False)
```

```python
import functools

import jax
import jax.numpy as jnp
from jax import lax
from jax.experimental import pallas as pl
from jax.experimental.pallas import tpu as pltpu
from jax.sharding import Mesh
from jax.sharding import PartitionSpec as P

BLK = 128
NB = 8
COLS = NB * BLK
bf16 = jnp.bfloat16
f32 = jnp.float32
i32 = jnp.int32

VM = pl.BlockSpec(memory_space=pltpu.VMEM)
SM = pl.BlockSpec(memory_space=pltpu.SMEM)
HBM = pl.BlockSpec(memory_space=pltpu.HBM)
MIB = 1024 * 1024
NT = (((1,), (1,)), ((), ()))


def call(kernel, outs, ins, scratch=(), flops=0, data=0, grant=16, specs=None):
    made = pl.pallas_call(
        kernel,
        out_shape=outs,
        in_specs=ins,
        out_specs=specs or [VM] * len(outs),
        scratch_shapes=list(scratch),
        compiler_params=pltpu.CompilerParams(vmem_limit_bytes=grant * MIB),
        cost_estimate=pl.CostEstimate(flops=flops, bytes_accessed=data, transcendentals=0),
    )

    def run(*args):
        args = [pltpu.with_memory_space_constraint(a, pltpu.HBM) if i is HBM else a for a, i in zip(args, ins)]
        return made(*args)

    return run


def cols_at(i):
    return pl.ds(pl.multiple_of(i * BLK, BLK), BLK)


def rows_at(i, n):
    return pl.ds(pl.multiple_of(i * n, n), n)


def copies_of(pairs, sem):
    out = [pltpu.make_async_copy(a, b, sem.at[i]) for i, (a, b) in enumerate(pairs)]
    for c in out:
        c.start()
    return out


def entry_kernel(
    innov, cell, order, anom, loc, tang, spread, up, down, piece, own, innov_v, cell_v, order_s, edge, ends, tang_v, sem
):
    co = lax.axis_index("co")
    cells = anom.shape[0]
    n = loc.shape[0]
    h = piece.shape[0]
    copies = copies_of(
        (
            (innov, innov_v),
            (cell, cell_v),
            (order, order_s),
            (anom.at[pl.ds(cells - BLK, BLK)], edge.at[0]),
            (anom.at[pl.ds(0, BLK)], edge.at[1]),
            (loc.at[n - 1, 2], ends.at[0]),
            (loc.at[0, 0], ends.at[1]),
            (anom.at[rows_at(co, h)], piece),
            (tang, tang_v),
        ),
        sem,
    )
    for c in copies[:3]:
        c.wait()
    x = innov_v[...]
    hi = x.astype(bf16)
    mid = (x - hi.astype(f32)).astype(bf16)
    lo = (x - hi.astype(f32) - mid.astype(f32)).astype(bf16)
    rows = jnp.concatenate([hi, mid, lo, jnp.zeros((5, x.shape[1]), bf16)], axis=0)
    ids = lax.broadcasted_iota(i32, (cells, 1), 0)
    hit = jnp.where(ids == cell_v[...], 1.0, 0.0).astype(bf16)
    y = lax.dot_general(rows, hit, NT, preferred_element_type=f32)
    w = y[0:1] + y[1:2] + y[2:3]
    lane = lax.broadcasted_iota(i32, (8, BLK), 1)
    tag = jnp.zeros((8, BLK), f32)
    for i in range(NB):
        tag = jnp.where(lane == i, order_s[0, i].astype(f32), tag)
    one = jnp.concatenate([w[:, i * BLK : (i + 1) * BLK] for i in range(cells // BLK)] + [tag], axis=0)
    for k in range(spread.shape[0]):
        spread[k] = one
    for c in copies[3:]:
        c.wait()
    half = edge.shape[2]
    for j, out in enumerate((up, down)):
        out[:, :half] = edge[j]
        out[:, half:] = ends[j]
    own[...] = tang_v[...].astype(bf16)


def choose_kernel(own, oth, recv, traj, *refs):
    *outs, ints, order_s, sem = refs
    z = lax.axis_index("z")
    co = lax.axis_index("co")
    steps = recv.shape[0]
    nz = steps // 2
    for k in range(steps):
        ints[k : k + 1] = recv[k, 8:9, :].astype(i32)
    d = pltpu.make_async_copy(ints, order_s, sem)
    d.start()
    d.wait()
    at = [jnp.int32(q) for q in range(NB)]
    for t in range(steps - 1, -1, -1):
        for q in range(NB):
            traj[t + 1, q] = at[q]
        at = [order_s[t, b] for b in at]
    for q in range(NB):
        traj[0, q] = at[q]
    for d, out in enumerate(outs):
        q = lax.rem(jnp.where(co == 0, z + d, z + nz - d), nz)
        mine = own[traj[2 * z + co + 1, q]]
        if d < nz // 2:
            out[co] = mine
            out[1 - co] = oth[traj[2 * z + 2 - co, q]]
        else:
            out[...] = mine


def ready_kernel(anom, loc, lt, gown, asel, anom_v, loc_v, held, sem, out_sem):
    co = lax.axis_index("co")
    copies = copies_of(((loc, loc_v), (anom, anom_v)), sem)
    n = loc.shape[0]
    half = anom.shape[1]
    none = jnp.zeros((BLK, BLK), bf16)
    copies[0].wait()
    for b in range(n):
        prev = none if b == 0 else loc_v[b - 1, 2].T
        nxt = none if b == n - 1 else loc_v[b + 1, 0].T
        lt[b] = jnp.concatenate([prev, loc_v[b, 1].T, nxt], axis=1)
    copies[1].wait()
    held[:BLK] = jnp.zeros((BLK, half), bf16)
    held[(n - 1) * BLK :] = jnp.zeros((BLK, half), bf16)
    for b in range(1, n - 1):
        y = jnp.dot(lt[b], anom_v[(b - 1) * BLK : (b + 2) * BLK], preferred_element_type=f32)
        held[b * BLK : (b + 1) * BLK] = y.astype(bf16)
    sent = pltpu.make_async_copy(held, gown, out_sem)
    sent.start()
    at = anom_v[...].T
    for k in range(half // 64):
        asel[k * 32 : (k + 1) * 32] = jnp.where(co == 0, at[k * 64 : k * 64 + 32], at[k * 64 + 32 : (k + 1) * 64])
    sent.wait()


def product_kernel(
    scale,
    near,
    far,
    anom,
    gown,
    up0,
    up1,
    down0,
    down1,
    lt,
    asel,
    recv,
    out,
    pad,
    full,
    vals,
    wt,
    res,
    ends,
    ints,
    order_s,
    sem,
    out_sem,
):
    co = lax.axis_index("co")
    e = lax.axis_index("ens")
    z = lax.axis_index("z")
    steps = recv.shape[0]
    for k in range(steps):
        ints[k : k + 1] = recv[k, 8:9, :].astype(i32)
    cells, half = anom.shape
    n = lt.shape[0]
    here = pl.ds(pl.multiple_of(e * half, half), half)
    there = pl.ds(pl.multiple_of((1 - e) * half, half), half)

    h = near.shape[0]
    copies = copies_of(
        (
            (near, pad.at[pl.ds(pl.multiple_of(BLK + co * h, BLK), h)]),
            (far, pad.at[pl.ds(pl.multiple_of(BLK + (1 - co) * h, BLK), h)]),
            (anom.at[pl.ds(0, 2 * BLK)], ends.at[0]),
            (anom.at[pl.ds(cells - 2 * BLK, 2 * BLK)], ends.at[1]),
            (ints, order_s),
            (gown, full.at[:, here]),
        ),
        sem,
    )
    blank = jnp.zeros((BLK - steps, BLK), f32)
    for b in range(n):
        wt[b * BLK : (b + 1) * BLK] = jnp.concatenate([recv[:, b, :], blank], axis=0).T
    first = jnp.concatenate([up0[:, half:].T, lt[0, :, BLK:]], axis=1)
    final = jnp.concatenate([lt[n - 1, :, : 2 * BLK], down0[:, half:].T], axis=1)
    pad[:BLK] = jnp.where(co == 0, up1[:, :half], up0[:, :half])
    pad[BLK + cells :] = jnp.where(co == 0, down1[:, :half], down0[:, :half])
    copies[0].wait()
    copies[1].wait()
    for b in range(n):
        left = first if b == 0 else final if b == n - 1 else lt[b]
        y = jnp.dot(left, pad[b * BLK : (b + 3) * BLK], preferred_element_type=f32)
        full[b * BLK : (b + 1) * BLK, there] = y.astype(bf16)
    copies[2].wait()
    copies[3].wait()
    top = jnp.concatenate([jnp.where(co == 0, up0[:, :half], up1[:, :half]), ends[0]], axis=0)
    low = jnp.concatenate([ends[1], jnp.where(co == 0, down0[:, :half], down1[:, :half])], axis=0)
    top = jnp.dot(first, top, preferred_element_type=f32).astype(bf16)
    low = jnp.dot(final, low, preferred_element_type=f32).astype(bf16)
    copies[4].wait()
    copies[5].wait()
    full[:BLK, here] = top
    full[cells - BLK :, here] = low
    at = [None] * steps
    b = z
    for t in range(steps - 1, -1, -1):
        at[t] = cols_at(b)
        b = order_s[t, b]
    for t in range(steps):
        w = jnp.broadcast_to(wt[:, t : t + 1], (n * BLK, BLK)).astype(bf16)
        vals[:, t * BLK : (t + 1) * BLK] = w * full[:, at[t]]
    sent = []
    width = steps * BLK // out_sem.shape[0]
    for g in range(out_sem.shape[0]):
        cols = slice(g * width, (g + 1) * width)
        y = jnp.dot(asel[...], vals[:, cols], preferred_element_type=f32)
        res[:, cols] = (y * scale).astype(bf16)
        c = pltpu.make_async_copy(res.at[:, cols], out.at[:, cols], out_sem.at[g])
        c.start()
        sent.append(c)
    for c in sent:
        c.wait()


def split(x):
    hi = x.astype(bf16)
    lo = (x - hi.astype(f32)).astype(bf16)
    return jnp.concatenate([hi, lo], axis=0)


def times(x, block, transposed):
    dims = NT if transposed else (((1,), (0,)), ((), ()))
    y = lax.dot_general(split(x), block, dims, preferred_element_type=f32)
    rows = x.shape[0]
    return y[:rows] + y[rows:]


def pack_kernel(*refs):
    *got, out = refs
    for j, src in enumerate(got[:-1]):
        out[2 * j : 2 * j + 2] = src[...]
    out[2 * len(got) - 2] = got[-1][...]


def scan_kernel(parts, own, mine, theirs, out, blocks):
    co = lax.axis_index("co")
    z = lax.axis_index("z")
    n = parts.shape[0]
    steps = parts.shape[2] // BLK
    nz = steps // 2
    h = nz // 2
    blocks[pl.ds(2 * z, 2)] = own[...]
    for d in range(1, h):
        for src, back in ((mine, co == 0), (theirs, co == 1)):
            k = lax.rem(jnp.where(back, z + nz - d, z + d), nz)
            blocks[pl.ds(2 * k, 2)] = src[2 * d - 2 : 2 * d]
    k = lax.rem(z + h, nz)
    blocks[2 * k + co] = mine[2 * h - 2]
    blocks[2 * k + 1 - co] = theirs[2 * h - 2]
    force = []
    for t in range(steps):
        at = slice(t * BLK, (t + 1) * BLK)
        y = parts[0, :, at].astype(f32)
        for s in range(1, n):
            y = y + parts[s, :, at].astype(f32)
        force.append(y)
    x = force[0]
    y = times(force[steps - 1], blocks[steps - 1], False)
    out[0, 0] = x.astype(bf16)
    out[steps - 1, 1] = y.astype(bf16)
    for k in range(1, steps):
        t = steps - 1 - k
        x = times(x, blocks[k], True) + force[k]
        y = times(y + force[t], blocks[t], False)
        out[k, 0] = x.astype(bf16)
        out[t, 1] = y.astype(bf16)


def place_kernel(recv, traj, x, y, xs, ys, sem):
    t = 2 * lax.axis_index("z") + lax.axis_index("co")
    rows = recv.shape[2]
    sent = []
    for j, (to, held) in enumerate(((x, xs), (y, ys))):
        for q in range(NB):
            at = cols_at(traj[t + 1 - j, q])
            for c in range(2):
                held[0, c * rows : (c + 1) * rows, at] = recv[2 * q + c, j].astype(f32)
        c = pltpu.make_async_copy(held, to, sem.at[j])
        c.start()
        sent.append(c)
    for c in sent:
        c.wait()


def on_device(anomalies, localization, innovations, obs_cell, tangent_blocks, tangent_order):
    cells, half = anomalies.shape
    n_lon = lax.axis_size("lon")
    nz = lax.axis_size("z")
    steps = 2 * nz
    shape = jax.ShapeDtypeStruct
    swap = [(0, 1), (1, 0)]
    scale = float(cells * n_lon) ** (-0.5)
    n = cells // BLK
    time = ("z", "co")

    spread, tail, head, piece, own_blocks = call(
        entry_kernel,
        [
            shape((steps, 16, BLK), f32),
            shape((BLK, half + BLK), bf16),
            shape((BLK, half + BLK), bf16),
            shape((cells // 2, half), bf16),
            shape((NB, BLK, BLK), bf16),
        ],
        [HBM] * 6,
        [
            pltpu.VMEM(innovations.shape, f32),
            pltpu.VMEM(obs_cell.shape, i32),
            pltpu.SMEM(tangent_order.shape, i32),
            pltpu.VMEM((2, BLK, half), bf16),
            pltpu.VMEM((2, BLK, BLK), bf16),
            pltpu.VMEM((NB, BLK, BLK), f32),
            pltpu.SemaphoreType.DMA((9,)),
        ],
        flops=10**7,
        data=10**6,
    )(innovations, obs_cell, tangent_order, anomalies, localization, tangent_blocks.reshape(NB, BLK, BLK))

    upward, downward = [], []
    for c in range(2):
        for k in range(n_lon):
            for e in range(2):
                f = e if c == 0 else 1 - e
                k2 = (k + 1) % n_lon
                upward.append(((c * n_lon + k) * 2 + e, (c * n_lon + k2) * 2 + f))
                downward.append(((c * n_lon + k2) * 2 + e, (c * n_lon + k) * 2 + f))
    up0 = lax.ppermute(tail, ("co", "lon", "ens"), upward)
    down0 = lax.ppermute(head, ("co", "lon", "ens"), downward)
    near = lax.ppermute(piece, "ens", swap)
    recv = lax.all_to_all(spread, time, 0, 0, tiled=True)
    oth_blocks = lax.ppermute(own_blocks, "co", swap)
    traj, *sends = call(
        choose_kernel,
        [shape((steps + 1, NB), i32)] + [shape((2, BLK, BLK), bf16)] * (nz // 2) + [shape((BLK, BLK), bf16)],
        [VM] * 3,
        [pltpu.VMEM((steps, BLK), i32), pltpu.SMEM((steps, BLK), i32), pltpu.SemaphoreType.DMA],
        flops=10**6,
        data=10**6,
        specs=[SM] + [VM] * (nz // 2 + 1),
        grant=4,
    )(own_blocks, oth_blocks, recv)
    got = []
    for d in range(1, nz // 2):
        pairs = []
        for k in range(nz):
            pairs.append((2 * k, (k + d) % nz * 2))
            pairs.append((2 * k + 1, (k - d) % nz * 2 + 1))
        got.append(lax.ppermute(sends[d], time, pairs))
    last = lax.ppermute(sends[nz // 2], "z", [(k, (k + nz // 2) % nz) for k in range(nz)])
    (mine,) = call(pack_kernel, [shape((nz - 1, BLK, BLK), bf16)], [VM] * (nz // 2), data=10**6)(*got, last)
    theirs = lax.ppermute(mine, "co", swap)

    up1 = lax.ppermute(up0, "co", swap)
    down1 = lax.ppermute(down0, "co", swap)
    lt, gown, asel = call(
        ready_kernel,
        [
            shape((n, BLK, 3 * BLK), bf16),
            pltpu.HBM((cells, half), bf16),
            shape((half // 2, cells), bf16),
        ],
        [HBM, HBM],
        [
            pltpu.VMEM(anomalies.shape, bf16),
            pltpu.VMEM(localization.shape, bf16),
            pltpu.VMEM((cells, half), bf16),
            pltpu.SemaphoreType.DMA((2,)),
            pltpu.SemaphoreType.DMA,
        ],
        flops=10**9,
        data=4 * 10**6,
        specs=[VM, HBM, VM],
        grant=10,
    )(anomalies, localization)
    far = lax.ppermute(near, "co", swap)
    (prod,) = call(
        functools.partial(product_kernel, scale),
        [shape((half // 2, steps * BLK), bf16)],
        [HBM, VM, HBM, HBM] + [VM] * 7,
        [
            pltpu.VMEM((cells + 2 * BLK, half), bf16),
            pltpu.VMEM((cells, COLS), bf16),
            pltpu.VMEM((cells, steps * BLK), bf16),
            pltpu.VMEM((cells, BLK), f32),
            pltpu.VMEM((half // 2, steps * BLK), bf16),
            pltpu.VMEM((2, 2 * BLK, half), bf16),
            pltpu.VMEM((steps, BLK), i32),
            pltpu.SMEM((steps, BLK), i32),
            pltpu.SemaphoreType.DMA((6,)),
            pltpu.SemaphoreType.DMA((2,)),
        ],
        flops=10**9,
        data=4 * 10**6,
        grant=16,
        specs=[HBM],
    )(near, far, anomalies, gown, up0, up1, down0, down1, lt, asel, recv)
    rows = half // 2 // n_lon
    parts = lax.all_to_all(prod, "lon", 0, 0, tiled=True).reshape(n_lon, rows, steps * BLK)
    (states,) = call(
        scan_kernel,
        [shape((steps, 2, rows, BLK), bf16)],
        [VM] * 4,
        [pltpu.VMEM((steps, BLK, BLK), bf16)],
        flops=10**9,
        data=2 * 10**6,
    )(parts, sends[0], mine, theirs)
    back = lax.all_to_all(states, time, 0, 0, tiled=True)
    x, y = call(
        place_kernel,
        [shape((1, 2 * rows, COLS), f32)] * 2,
        [VM, SM],
        [pltpu.VMEM((1, 2 * rows, COLS), f32), pltpu.VMEM((1, 2 * rows, COLS), f32), pltpu.SemaphoreType.DMA((2,))],
        flops=10**6,
        data=10**6,
        specs=[HBM, HBM],
    )(back, traj)
    return x, y


def solution(mesh):
    tm, lon, ens = (mesh.shape[a] for a in ("tm", "lon", "ens"))
    fine = Mesh(mesh.devices.reshape(tm // 2, 2, lon, ens), ("z", "co", "lon", "ens"))
    time = ("z", "co")
    placed = (
        P("lon", "ens"),
        P("lon", None, None, None),
        P(time, "lon"),
        P(time, "lon"),
        P(time, None, None, None),
        P(time, None),
    )
    outs = P(time, ("ens", "lon"), None)

    return jax.shard_map(on_device, mesh=fine, in_specs=placed, out_specs=(outs, outs), check_vma=False)
```
